512 devices in a mesh: gz: 8 (over y, core), xy: 64 (over x, z).
Axes of the slice: x: 4, y: 4, z: 16, core: 2. Of those that a mesh axis runs over, the one named last changes fastest.
Arguments:
- velocity_free: float32 [8, 64, 6, 512], P('gz', 'xy'), may hold values from -6 to 6
- inverse_mass: float32 [8, 64, 2, 512], P('gz', 'xy'), may hold values from 0.25 to 4
- jacobian: float32 [8, 64, 36, 2048], P('gz', 'xy'), may hold values from -1.75 to 1.75
- impulses: float32 [8, 64, 3, 2048], P('gz', 'xy'), may hold values from -6 to 6
- previous_impulses: float32 [8, 64, 3, 2048], P('gz', 'xy'), may hold values from -6 to 6
- compliance: float32 [8, 64, 2048], P('gz', 'xy'), may hold values from 0.05 to 0.5
- offset: float32 [8, 64, 2048], P('gz', 'xy'), may hold values from -6 to 6
- friction: float32 [8, 64, 2048], P('gz', 'xy'), may hold values from 0.2 to 0.8
- body_near: int32 [8, 64, 2048], P('gz', 'xy'), may hold values from 0 to 511
- body_far: int32 [8, 64, 2048], P('gz', 'xy'), may hold values from 0 to 1023
- block_counts: int32 [8, 64, 16], P('gz', 'xy'), may hold values from 0 to 128, as said below
- layer_send: int32 [8, 64, 128], P('gz', 'xy'), may hold values from 0 to 511
- side_send: int32 [8, 64, 2, 192], P('gz', 'xy'), may hold values from 0 to 639
Outputs:
- impulses_out: float32 [8, 64, 3, 2048], P('gz', 'xy')
- velocity_out: float32 [8, 64, 6, 512], P('gz', 'xy')
The draws below stay inside these ranges and needn't reach their ends.
Inputs may be any that keep to these rules, and one draw needn't show every extreme that they name: `block_counts`: on each device the blocks that hold live contacts come first, every one of them but the last full; some device holds 2048 live contacts. `body_far`: entries of 512 or more name received rows: 512 + i is the row received as the i-th from the layer above, then 192 rows from the lower-side and 192 from the higher-side neighbour. `side_send`: entries of 512 or more name rows received from the layer above.
All inputs are finite; a program needn't handle non-finite values.
Results may differ from the reference program's by a relative error of at most 0.0003.
Values sent between devices are 32-bit elements; how exact they have to be, the bound alone decides.
A program may use at most 64 MiB of HBM per device.

```python
import math
import jax
import jax.numpy as jnp
from jax import lax

CB = 16
BLOCK = 128
ITERS = 2
LAYERS = 8
CELLS = 64
CON = 2048
SPH = 512
GZS = 128
XS = 192
EXT = 1024


def draw_block_counts(key, part):
    factor_key, chosen_key = jax.random.split(key, 2)
    layer_index = jnp.arange(LAYERS, dtype=jnp.int32)[:, None]
    cell_index = jnp.arange(CELLS, dtype=jnp.int32)[None, :]
    layer_total = CON * (3 * (LAYERS - 1) - 2 * layer_index) // (3 * (LAYERS - 1))
    random_root = jax.random.randint(factor_key, (LAYERS, CELLS), 0, 17)
    live_total = layer_total * (256 + 3 * random_root * random_root) // 1024
    chosen_cell = jax.random.randint(chosen_key, (), 0, CELLS)
    live_total = jnp.where((layer_index == 0) & (cell_index == chosen_cell), CON, live_total)
    slot_excess = live_total[:, :, None] - BLOCK * jnp.arange(CB, dtype=jnp.int32)[None, None, :]
    return jnp.clip(slot_excess, 0, BLOCK).astype(jnp.int32)


def plant(values, stream_key, low, top_value):
    shape = values.shape
    index_at = [jax.random.randint(jax.random.fold_in(stream_key, axis), (), 0, shape[axis]) for axis in range(len(shape))]
    values = values.at[tuple(index_at)].set(low)
    longest = shape.index(max(shape))
    index_at[longest] = (index_at[longest] + 1) % shape[longest]
    return values.at[tuple(index_at)].set(top_value)


def block_scale(rng, dims, cuts, least, top_value):
    gain = 1.0
    for dim, shards_of in cuts:
        steps = jax.random.uniform(jax.random.fold_in(jax.random.fold_in(rng, 6), dim), (shards_of,), jnp.float32, least / len(cuts), top_value / len(cuts))
        gain = gain * jnp.repeat(jnp.exp(steps), dims[dim] // shards_of).reshape((-1,) + (1,) * (len(dims) - 1 - dim))
    return gain


def scatter_about(stream_key, shape, width, most, pieces=(), kind=jnp.bfloat16):
    loudness = block_scale(stream_key, shape, pieces, -0.22, 0.18) if pieces else 1.0
    values = jax.random.normal(stream_key, shape, jnp.float32) * width * loudness
    return jnp.minimum(jnp.maximum(values, -most), most).astype(kind)


def setup_inputs(seed: int = 0) -> dict:
    splits = jax.random.split(jax.random.key(seed), 14)
    velocity_free = scatter_about(splits[0], (LAYERS, CELLS, 6, SPH), 1.0, 6.0, ((0, 8), (1, 64)), jnp.float32)
    inverse_mass = jnp.clip(jnp.exp(math.log(4.0) - 2.7725887 * jax.random.uniform(splits[1], (LAYERS, CELLS, 2, SPH), jnp.float32) ** block_scale(splits[1], (LAYERS, CELLS, 2, SPH), ((0, 8), (1, 64)), -0.2, 0.2)), 0.25, 4.0)
    jacobian = scatter_about(splits[2], (LAYERS, CELLS, 36, CON), 12 ** -0.5, 1.75, ((0, 8), (1, 64)), jnp.float32)
    impulses = scatter_about(splits[3], (LAYERS, CELLS, 3, CON), 1.0, 6.0, ((0, 8), (1, 64)), jnp.float32)
    previous_impulses = scatter_about(splits[4], (LAYERS, CELLS, 3, CON), 1.0, 6.0, ((0, 8), (1, 64)), jnp.float32)
    compliance = jnp.clip(jnp.exp(math.log(0.5) - 2.3025851 * jax.random.uniform(splits[5], (LAYERS, CELLS, CON), jnp.float32) ** block_scale(splits[5], (LAYERS, CELLS, CON), ((0, 8), (1, 64)), -0.2, 0.2)), 0.05, 0.5)
    offset = scatter_about(splits[6], (LAYERS, CELLS, CON), 1.0, 6.0, ((0, 8), (1, 64)), jnp.float32)
    friction = jnp.clip(jnp.exp(math.log(0.8) - 1.3862944 * jax.random.uniform(splits[7], (LAYERS, CELLS, CON), jnp.float32) ** block_scale(splits[7], (LAYERS, CELLS, CON), ((0, 8), (1, 64)), -0.2, 0.2)), 0.2, 0.8)
    body_near = plant(jax.random.randint(splits[8], (LAYERS, CELLS, CON), 0, SPH), jax.random.fold_in(splits[8], 1), 0, SPH - 1).astype(jnp.int32)
    body_far = plant(jax.random.randint(splits[9], (LAYERS, CELLS, CON), 0, EXT), jax.random.fold_in(splits[9], 1), 0, EXT - 1).astype(jnp.int32)
    block_counts = draw_block_counts(jax.random.fold_in(splits[13], 71), 0)
    layer_send = plant(jax.random.randint(splits[11], (LAYERS, CELLS, GZS), 0, SPH), jax.random.fold_in(splits[11], 1), 0, SPH - 1).astype(jnp.int32)
    side_send = plant(jax.random.randint(splits[12], (LAYERS, CELLS, 2, XS), 0, SPH + GZS), jax.random.fold_in(splits[12], 1), 0, (SPH + GZS) - 1).astype(jnp.int32)
    return {"velocity_free": velocity_free, "inverse_mass": inverse_mass, "jacobian": jacobian, "impulses": impulses, "previous_impulses": previous_impulses, "compliance": compliance, "offset": offset, "friction": friction, "body_near": body_near, "body_far": body_far, "block_counts": block_counts, "layer_send": layer_send, "side_send": side_send}


EPSILON = 1e-06
THETA_START = 0.3

def theta_after(theta_value):
    return 0.5 * (-theta_value * theta_value + theta_value * math.sqrt(theta_value * theta_value + 4.0))

def momentum_factors(iteration_count):
    thetas = [THETA_START]
    for iteration in range(iteration_count):
        thetas.append(theta_after(thetas[-1]))
    return [thetas[position] * (1.0 - thetas[position]) / (thetas[position] * thetas[position] + thetas[position + 1]) for position in range(iteration_count)]

def contact_rows(jacobian_dev, extended, near_index, far_index):
    blocks = jacobian_dev.reshape(3, 12, -1)
    near_rows = extended[:, near_index]
    far_rows = extended[:, far_index]
    return lax.optimization_barrier(jnp.sum(blocks[:, :6] * near_rows[None], axis=1)) + lax.optimization_barrier(jnp.sum(blocks[:, 6:] * far_rows[None], axis=1))

def sphere_terms(jacobian_dev, impulse, near_index, far_index, base_terms):
    blocks = jacobian_dev.reshape(3, 12, -1)
    spread = lax.optimization_barrier(jnp.sum(blocks * impulse[:, None], axis=0))
    return base_terms.at[:, near_index].add(spread[:6]).at[:, far_index].add(spread[6:])

def cone_project(impulse_value, cone_friction):
    normal = impulse_value[0]
    tangent = impulse_value[1:]
    slide_norm = jnp.sqrt(tangent[0] * tangent[0] + tangent[1] * tangent[1])
    inside_cone = slide_norm <= cone_friction * normal
    polar_cone = cone_friction * slide_norm <= -normal
    outside_both = jnp.logical_not(jnp.logical_or(inside_cone, polar_cone))
    onto_normal = (cone_friction * slide_norm + normal) / (cone_friction * cone_friction + 1.0)
    tangent_scale = cone_friction * onto_normal / jnp.where(outside_both, slide_norm, 1.0)
    new_normal = jnp.where(inside_cone, normal, jnp.where(polar_cone, 0.0, onto_normal))
    new_tangent = jnp.where(inside_cone[None], tangent, jnp.where(polar_cone[None], 0.0, tangent_scale[None] * tangent))
    return jnp.concatenate([new_normal[None], new_tangent], axis=0)

def take_columns(field, index_list):
    return field[:, index_list]

def add_columns(base_terms, values, index_list):
    return base_terms.at[:, index_list].add(values)

def spread_field(field, layer_send, side_send):
    take = jax.vmap(jax.vmap(take_columns))
    upper_rows = take(field, layer_send)
    upper_rows = jnp.concatenate([upper_rows[1:], jnp.zeros_like(upper_rows[:1])], axis=0)
    first_section = jnp.concatenate([field, upper_rows], axis=3)
    to_lower = take(first_section, side_send[:, :, 0])
    to_higher = take(first_section, side_send[:, :, 1])
    from_lower = jnp.concatenate([jnp.zeros_like(to_higher[:, :1]), to_higher[:, :-1]], axis=1)
    from_higher = jnp.concatenate([to_lower[:, 1:], jnp.zeros_like(to_lower[:, :1])], axis=1)
    return jnp.concatenate([first_section, from_lower, from_higher], axis=3)

def collect_terms(terms, layer_send, side_send):
    place = jax.vmap(jax.vmap(add_columns))
    section_rows = SPH + GZS
    first_section = terms[..., :section_rows]
    lower_part = terms[..., section_rows:section_rows + XS]
    higher_part = terms[..., section_rows + XS:]
    from_higher_cell = jnp.concatenate([lower_part[:, 1:], jnp.zeros_like(lower_part[:, :1])], axis=1)
    from_lower_cell = jnp.concatenate([jnp.zeros_like(higher_part[:, :1]), higher_part[:, :-1]], axis=1)
    first_section = place(first_section, from_higher_cell, side_send[:, :, 1])
    first_section = place(first_section, from_lower_cell, side_send[:, :, 0])
    layer_part = first_section[..., SPH:]
    from_below = jnp.concatenate([jnp.zeros_like(layer_part[:1]), layer_part[:-1]], axis=0)
    return place(first_section[..., :SPH], from_below, layer_send)

def reference(velocity_free, inverse_mass, jacobian, impulses, previous_impulses, compliance, offset, friction, body_near, body_far, block_counts, layer_send, side_send):
    device_count = LAYERS * CELLS

    def per_device(function, *arrays):
        flat = tuple((array.reshape((device_count,) + array.shape[2:]) for array in arrays))
        result = lax.map(lambda parts: function(*parts), flat)
        return result.reshape((LAYERS, CELLS) + result.shape[1:])

    def terms_dev(jacobian_dev, impulse_dev, near_dev, far_dev):
        return sphere_terms(jacobian_dev, impulse_dev, near_dev, far_dev, jnp.zeros((6, EXT), jnp.float32))
    weights = jnp.concatenate([jnp.repeat(inverse_mass[:, :, 0:1], 3, axis=2), jnp.repeat(inverse_mass[:, :, 1:2], 3, axis=2)], axis=2)
    slot_index = (jnp.arange(CON, dtype=jnp.int32) % BLOCK)[None, None, :]
    alive = (slot_index < jnp.repeat(block_counts, BLOCK, axis=2)).astype(jnp.float32)[:, :, None]
    zeros_rows = jnp.zeros_like(offset)
    offset_rows = jnp.stack([offset, zeros_rows, zeros_rows], axis=2)
    softness = compliance[:, :, None]

    def velocity_of(impulse):
        terms = per_device(terms_dev, jacobian, impulse, body_near, body_far)
        return velocity_free + weights * collect_terms(terms, layer_send, side_send)
    factors = momentum_factors(ITERS)
    current = alive * impulses
    earlier = alive * previous_impulses
    guess = alive * (current + factors[0] * (current - earlier))
    for iteration in range(ITERS):
        extended = spread_field(velocity_of(guess), layer_send, side_send)
        rows_now = per_device(contact_rows, jacobian, extended, body_near, body_far)
        gradient = alive * (rows_now + offset_rows + softness * guess)
        sphere_sums = collect_terms(per_device(terms_dev, jacobian, gradient, body_near, body_far), layer_send, side_send)
        norm_sq = jnp.sum(gradient * gradient)
        curvature = jnp.sum(weights * sphere_sums * sphere_sums) + jnp.sum(softness * gradient * gradient)
        step_size = norm_sq / (curvature + EPSILON)
        updated = alive * per_device(cone_project, guess - step_size * gradient, friction)
        if iteration + 1 < ITERS:
            guess = alive * (updated + factors[iteration + 1] * (updated - current))
        current = updated
    return (current, velocity_of(current))
```

```python
import functools
import math

import jax
import jax.numpy as jnp
from jax import lax
from jax.experimental import pallas as pl
from jax.experimental.pallas import tpu as pltpu
from jax.sharding import PartitionSpec as P

ITERS = 2
EPSILON = 1e-06
THETA_START = 0.3

MESH = pl.DeviceIdType.MESH
F32 = jnp.float32
BF16 = jnp.bfloat16
WIDE = 256
PHASES = 3 * ITERS + 1
GROUP = 8
ROUNDS = 3


def theta_after(theta_value):
    return 0.5 * (
        -theta_value * theta_value + theta_value * math.sqrt(theta_value * theta_value + 4.0)
    )


def momentum_factors(iteration_count):
    thetas = [THETA_START]
    for iteration in range(iteration_count):
        thetas.append(theta_after(thetas[-1]))
    return [
        thetas[position]
        * (1.0 - thetas[position])
        / (thetas[position] * thetas[position] + thetas[position + 1])
        for position in range(iteration_count)
    ]


def halves(rows):
    high = rows.astype(BF16).astype(F32)
    return jnp.concatenate([high, rows - high], axis=0).astype(BF16)


def set_hot(index, hot_ref, mask_ref):
    lane = jnp.where(index < 0, -1, index & (WIDE - 1))
    tile = index >> 8
    width = index.shape[1]
    for start in range(0, width, WIDE):
        part = lane[:, start : start + WIDE]
        row = lax.broadcasted_iota(jnp.int32, (WIDE, WIDE), 0)
        hot_ref[:, start : start + WIDE] = (row == part).astype(F32).astype(BF16)
    for number in range(mask_ref.shape[0]):
        mask = (tile == number).astype(F32)
        mask_ref[number] = jnp.broadcast_to(mask, (16, width)).astype(BF16)


def scatter(rows, hot_ref, mask_ref):
    both = halves(rows)
    tiles = mask_ref.shape[0]
    left = jnp.concatenate([both * mask_ref[number] for number in range(tiles)], axis=0)
    sums = lax.dot_general(
        left, hot_ref[...], (((1,), (1,)), ((), ())), preferred_element_type=F32
    )
    return [
        sums[16 * number : 16 * number + 8] + sums[16 * number + 8 : 16 * number + 16]
        for number in range(tiles)
    ]


def gather(tiles, numbers, hot_ref, mask_ref):
    left = jnp.concatenate([halves(tile) for tile in tiles], axis=0)
    found = jnp.dot(left, hot_ref[...], preferred_element_type=F32)
    total = None
    for position, number in enumerate(numbers):
        part = found[16 * position : 16 * position + 8] + found[16 * position + 8 : 16 * position + 16]
        part = part * mask_ref[number][:8].astype(F32)
        total = part if total is None else total + part
    return total


def lanes(row):
    total = row[:, :128]
    for start in range(128, row.shape[1], 128):
        total = total + row[:, start : start + 128]
    return total


def cone_project(normal, first, second, friction):
    slide = jnp.sqrt(first * first + second * second)
    inside = slide <= friction * normal
    polar = friction * slide <= -normal
    outside = jnp.logical_not(jnp.logical_or(inside, polar))
    onto = (friction * slide + normal) / (friction * friction + 1.0)
    scale = friction * onto / jnp.where(outside, slide, 1.0)
    scale = jnp.where(inside, 1.0, jnp.where(polar, 0.0, scale))
    new_normal = jnp.where(inside, normal, jnp.where(polar, 0.0, onto))
    return [new_normal, scale * first, scale * second]


def kernel(
    layers,
    cells,
    free_ref,
    mass_ref,
    jacobian_ref,
    impulses_ref,
    previous_ref,
    compliance_ref,
    offset_ref,
    friction_ref,
    near_ref,
    far_ref,
    counts_ref,
    layer_ref,
    side_ref,
    impulses_out,
    velocity_out,
    near_hot,
    near_mask,
    far_hot,
    far_mask,
    halo_hot,
    halo_mask,
    near_jac,
    far_jac,
    side_out,
    side_in,
    sent,
    received,
    sum_out,
    sum_in,
    side_sems,
    phase_send,
    phase_recv,
    sum_send,
    sum_recv,
):
    g = lax.axis_index("gz")
    x = lax.axis_index("xy")
    below, above = (g + layers - 1) % layers, (g + 1) % layers
    lower, higher = (x + cells - 1) % cells, (x + 1) % cells
    block = x // GROUP * GROUP
    peers = [
        [((g + step) % layers, x) for step in range(1, layers)],
        [(g, block + (x - block + step) % GROUP) for step in range(1, GROUP)],
        [(g, (x + GROUP * step) % cells) for step in range(1, cells // GROUP)],
    ]
    around = [
        (g, lower),
        (g, higher),
        (below, x),
        (above, x),
        (below, lower),
        (below, higher),
        (above, lower),
        (above, higher),
    ]

    barrier = pltpu.get_barrier_semaphore()
    greeted = around + peers[0] + peers[1] + peers[2]
    for device in greeted:
        pl.semaphore_signal(barrier, inc=1, device_id=device, device_id_type=MESH)

    def remote(src, dst, send_sem, recv_sem, device):
        copy = pltpu.make_async_remote_copy(
            src_ref=src,
            dst_ref=dst,
            send_sem=send_sem,
            recv_sem=recv_sem,
            device_id=device,
            device_id_type=MESH,
        )
        copy.start()

    near_jac[...] = jnp.zeros_like(near_jac)
    far_jac[...] = jnp.zeros_like(far_jac)
    for r in range(3):
        near_jac[r, 0:6, :] = jacobian_ref[12 * r : 12 * r + 6, :]
        far_jac[r, 0:6, :] = jacobian_ref[12 * r + 6 : 12 * r + 12, :]
    side_rows = side_ref.shape[1]
    side_list = side_ref[...].astype(F32)
    pad = jnp.full((1, WIDE - side_rows), -1.0, F32)
    side_row = jnp.concatenate([side_list[0:1], pad, side_list[1:2], pad], axis=1)
    side_out[...] = jnp.broadcast_to(side_row, side_out.shape)

    pl.semaphore_wait(barrier, len(greeted))
    remote(side_out, side_in, side_sems.at[0], side_sems.at[1], (above, x))

    own = free_ref.shape[1]
    layer_rows = layer_ref.shape[1]
    section = own + layer_rows
    far = far_ref[...]
    far = jnp.where(
        far < section, far, jnp.where(far < section + side_rows, far + (3 * WIDE - section), far + (4 * WIDE - section - side_rows))
    )
    set_hot(far, far_hot, far_mask)
    set_hot(near_ref[...], near_hot, near_mask)

    slot = lax.broadcasted_iota(jnp.int32, (1, 128), 1)
    alive = jnp.concatenate(
        [(slot < counts_ref[b]).astype(F32) for b in range(counts_ref.shape[0])], axis=1
    )
    softness = compliance_ref[...]
    friction = friction_ref[...]
    offset = offset_ref[...]
    sphere_row = lax.broadcasted_iota(jnp.int32, (8, own), 0)
    weights = jnp.where(
        sphere_row < 3, mass_ref[0:1, :], jnp.where(sphere_row < 6, mass_ref[1:2, :], 0.0)
    )
    free = jnp.concatenate([free_ref[...], jnp.zeros((2, own), F32)], axis=0)

    def set_halo():
        pltpu.make_async_copy(side_in, side_in, side_sems.at[1]).wait()
        layer = layer_ref[...]
        other = side_in[0:1, :].astype(jnp.int32)
        relative = other - own
        row = lax.broadcasted_iota(jnp.int32, (layer_rows, 2 * WIDE), 0)
        hot = (row == relative).astype(F32).astype(BF16)
        parts = jnp.concatenate(
            [jnp.broadcast_to(layer >> 8, (8, layer_rows)), jnp.broadcast_to(layer & 255, (8, layer_rows))], axis=0
        )
        found = jnp.dot(parts.astype(F32).astype(BF16), hot, preferred_element_type=F32)
        composed = (found[0:1] * 256.0 + found[8:9]).astype(jnp.int32)
        composed = jnp.where(relative >= 0, composed, -1)
        mine = side_row.astype(jnp.int32)
        mine = jnp.where(mine < own, mine, -1)
        bottom, first, last = g == 0, x == 0, x == cells - 1
        none = jnp.full((1, WIDE), -1, jnp.int32)
        to_layer = jnp.concatenate([layer, jnp.full((1, WIDE - layer_rows), -1, jnp.int32)], axis=1)
        index = jnp.concatenate(
            [
                jnp.where(bottom, none, to_layer),
                jnp.where(first, none, mine[:, :WIDE]),
                jnp.where(last, none, mine[:, WIDE:]),
                jnp.where(jnp.logical_or(bottom, first), none, composed[:, :WIDE]),
                jnp.where(jnp.logical_or(bottom, last), none, composed[:, WIDE:]),
            ],
            axis=1,
        )
        set_hot(index, halo_hot, halo_mask)

    def part(ref, phase, number):
        return ref.at[phase, :, pl.ds(number * WIDE, WIDE)]

    def arrive(phase):
        pltpu.make_async_copy(received.at[phase], received.at[phase], phase_recv.at[phase]).wait()

    def collect(phase, impulse, between=None):
        far_terms = far_jac[0] * impulse[0] + far_jac[1] * impulse[1] + far_jac[2] * impulse[2]
        far_tiles = scatter(far_terms, far_hot, far_mask)
        for number in range(3):
            sent[phase, :, number * WIDE : (number + 1) * WIDE] = far_tiles[2 + number]
        for number, segment, device in (
            (1, 2, (g, lower)),
            (2, 1, (g, higher)),
            (1, 4, (above, lower)),
            (2, 3, (above, higher)),
            (0, 0, (above, x)),
        ):
            remote(part(sent, phase, number), part(received, phase, segment), phase_send.at[phase], phase_recv.at[phase], device)
        near_terms = near_jac[0] * impulse[0] + near_jac[1] * impulse[1] + near_jac[2] * impulse[2]
        near_tiles = scatter(near_terms, near_hot, near_mask)
        if between is not None:
            between()
        arrive(phase)
        halo_tiles = scatter(received[phase], halo_hot, halo_mask)
        return jnp.concatenate(
            [far_tiles[i] + near_tiles[i] + halo_tiles[i] for i in range(2)], axis=1
        )

    def rows_of(phase, velocity):
        own_tiles = [velocity[:, :WIDE], velocity[:, WIDE:]]
        sent[phase] = gather(own_tiles, range(2), halo_hot, halo_mask)
        for segment, device in (
            (3, (below, lower)),
            (4, (below, higher)),
            (1, (g, lower)),
            (2, (g, higher)),
            (0, (below, x)),
        ):
            remote(part(sent, phase, segment), part(received, phase, segment), phase_send.at[phase], phase_recv.at[phase], device)
        near_rows = gather(own_tiles, range(2), near_hot, near_mask)
        far_rows = gather(own_tiles, range(2), far_hot, far_mask)
        partial = [near_jac[r] * near_rows for r in range(3)]
        arrive(phase)
        segments = [received[phase, :, i * WIDE : (i + 1) * WIDE] for i in range(5)]
        far_rows = far_rows + gather(
            [segments[0], segments[2] + segments[4], segments[1] + segments[3]], (2, 3, 4), far_hot, far_mask
        )
        return [
            jnp.sum(partial[r] + far_jac[r] * far_rows, axis=0, keepdims=True) for r in range(3)
        ]

    def all_sum(iteration, value):
        for number in range(ROUNDS):
            at = iteration * ROUNDS + number
            sum_out[at] = value
            for step, device in enumerate(peers[number]):
                remote(sum_out.at[at], sum_in.at[at, step], sum_send.at[at], sum_recv.at[at], device)
            pltpu.make_async_copy(sum_in.at[at], sum_in.at[at], sum_recv.at[at]).wait()
            for step in range(len(peers[number])):
                value = value + sum_in[at, step]
        return value

    factors = momentum_factors(ITERS)
    current = [alive * impulses_ref[r : r + 1, :] for r in range(3)]
    earlier = [alive * previous_ref[r : r + 1, :] for r in range(3)]
    guess = [alive * (current[r] + factors[0] * (current[r] - earlier[r])) for r in range(3)]
    for iteration in range(ITERS):
        phase = 3 * iteration
        velocity = free + weights * collect(phase, guess, set_halo if iteration == 0 else None)
        rows = rows_of(phase + 1, velocity)
        rows[0] = rows[0] + offset
        gradient = [alive * (rows[r] + softness * guess[r]) for r in range(3)]
        squares = gradient[0] * gradient[0] + gradient[1] * gradient[1] + gradient[2] * gradient[2]
        norm = lanes(squares)
        soft = lanes(softness * squares)
        sums = collect(phase + 2, gradient)
        curve = jnp.sum(lanes(weights * sums * sums), axis=0, keepdims=True) + soft
        tile_row = lax.broadcasted_iota(jnp.int32, (8, 128), 0)
        value = all_sum(iteration, jnp.where(tile_row == 0, norm, curve))
        total = jnp.sum(value, axis=1, keepdims=True)
        step_size = total[0:1] / (total[1:2] + EPSILON)
        moved = [guess[r] - step_size * gradient[r] for r in range(3)]
        updated = [alive * v for v in cone_project(moved[0], moved[1], moved[2], friction)]
        if iteration + 1 < ITERS:
            guess = [
                alive * (updated[r] + factors[iteration + 1] * (updated[r] - current[r]))
                for r in range(3)
            ]
        current = updated
    for r in range(3):
        impulses_out[r : r + 1, :] = current[r]
    final = free + weights * collect(PHASES - 1, current)
    velocity_out[...] = final[0:6, :]

    pltpu.make_async_copy(side_out, side_out, side_sems.at[0]).wait()
    for phase in range(PHASES):
        pltpu.make_async_copy(received.at[phase], received.at[phase], phase_send.at[phase]).wait()
    for at in range(ITERS * ROUNDS):
        pltpu.make_async_copy(sum_in.at[at], sum_in.at[at], sum_send.at[at]).wait()


def solution(mesh):
    layers, cells = mesh.shape["gz"], mesh.shape["xy"]

    def on_device(
        velocity_free,
        inverse_mass,
        jacobian,
        impulses,
        previous_impulses,
        compliance,
        offset,
        friction,
        body_near,
        body_far,
        block_counts,
        layer_send,
        side_send,
    ):
        own = velocity_free.shape[3]
        contacts = jacobian.shape[3]
        vmem = pl.BlockSpec(memory_space=pltpu.VMEM)
        smem = pl.BlockSpec(memory_space=pltpu.SMEM)
        sums = ITERS * ROUNDS
        outs = pl.pallas_call(
            functools.partial(kernel, layers, cells),
            out_shape=(
                jax.ShapeDtypeStruct((3, contacts), F32),
                jax.ShapeDtypeStruct((6, own), F32),
            ),
            in_specs=[vmem] * 10 + [smem] + [vmem] * 2,
            out_specs=(vmem, vmem),
            scratch_shapes=[
                pltpu.VMEM((WIDE, contacts), BF16),
                pltpu.VMEM((2, 16, contacts), BF16),
                pltpu.VMEM((WIDE, contacts), BF16),
                pltpu.VMEM((5, 16, contacts), BF16),
                pltpu.VMEM((WIDE, 5 * WIDE), BF16),
                pltpu.VMEM((2, 16, 5 * WIDE), BF16),
                pltpu.VMEM((3, 8, contacts), F32),
                pltpu.VMEM((3, 8, contacts), F32),
                pltpu.VMEM((8, 2 * WIDE), F32),
                pltpu.VMEM((8, 2 * WIDE), F32),
                pltpu.VMEM((PHASES, 8, 5 * WIDE), F32),
                pltpu.VMEM((PHASES, 8, 5 * WIDE), F32),
                pltpu.VMEM((sums, 8, 128), F32),
                pltpu.VMEM((sums, GROUP - 1, 8, 128), F32),
                pltpu.SemaphoreType.DMA((2,)),
                pltpu.SemaphoreType.DMA((PHASES,)),
                pltpu.SemaphoreType.DMA((PHASES,)),
                pltpu.SemaphoreType.DMA((sums,)),
                pltpu.SemaphoreType.DMA((sums,)),
            ],
            compiler_params=pltpu.CompilerParams(
                collective_id=0, has_side_effects=True, vmem_limit_bytes=40 << 20
            ),
        )(
            velocity_free[0, 0],
            inverse_mass[0, 0],
            jacobian[0, 0],
            impulses[0, 0],
            previous_impulses[0, 0],
            compliance[0],
            offset[0],
            friction[0],
            body_near[0],
            body_far[0],
            block_counts[0, 0],
            layer_send[0],
            side_send[0, 0],
        )
        return outs[0][None, None], outs[1][None, None]

    field = P("gz", "xy", None, None)
    line = P("gz", "xy", None)
    return jax.shard_map(
        on_device,
        mesh=mesh,
        in_specs=(field,) * 5 + (line,) * 7 + (field,),
        out_specs=(field, field),
        check_vma=False,
    )
```

```python
import functools
import math

import jax
import jax.numpy as jnp
from jax import lax
from jax.experimental import pallas as pl
from jax.experimental.pallas import tpu as pltpu
from jax.sharding import PartitionSpec as P

ITERS = 2
EPSILON = 1e-06
THETA_START = 0.3

MESH = pl.DeviceIdType.MESH
F32 = jnp.float32
BF16 = jnp.bfloat16
WIDE = 256
PHASES = 3 * ITERS + 1
ROUNDS = 2


def theta_after(theta_value):
    return 0.5 * (
        -theta_value * theta_value + theta_value * math.sqrt(theta_value * theta_value + 4.0)
    )


def momentum_factors(iteration_count):
    thetas = [THETA_START]
    for iteration in range(iteration_count):
        thetas.append(theta_after(thetas[-1]))
    return [
        thetas[position]
        * (1.0 - thetas[position])
        / (thetas[position] * thetas[position] + thetas[position + 1])
        for position in range(iteration_count)
    ]


def halves(rows):
    high = rows.astype(BF16).astype(F32)
    return jnp.concatenate([high, rows - high], axis=0).astype(BF16)


def set_hot(index, hot_ref, mask_ref):
    lane = jnp.where(index < 0, -1, index & (WIDE - 1))
    tile = index >> 8
    width = index.shape[1]
    for start in range(0, width, WIDE):
        part = lane[:, start : start + WIDE]
        row = lax.broadcasted_iota(jnp.int32, (WIDE, WIDE), 0)
        hot_ref[:, start : start + WIDE] = (row == part).astype(F32).astype(BF16)
    for number in range(mask_ref.shape[0]):
        mask = (tile == number).astype(F32)
        mask_ref[number] = jnp.broadcast_to(mask, (16, width)).astype(BF16)


def scatter(rows, hot_ref, mask_ref):
    both = halves(rows)
    tiles = mask_ref.shape[0]
    left = jnp.concatenate([both * mask_ref[number] for number in range(tiles)], axis=0)
    sums = lax.dot_general(
        left, hot_ref[...], (((1,), (1,)), ((), ())), preferred_element_type=F32
    )
    return [
        sums[16 * number : 16 * number + 8] + sums[16 * number + 8 : 16 * number + 16]
        for number in range(tiles)
    ]


def gather(tiles, numbers, hot_ref, mask_ref):
    left = jnp.concatenate([halves(tile) for tile in tiles], axis=0)
    found = jnp.dot(left, hot_ref[...], preferred_element_type=F32)
    total = None
    for position, number in enumerate(numbers):
        part = found[16 * position : 16 * position + 8] + found[16 * position + 8 : 16 * position + 16]
        part = part * mask_ref[number][:8].astype(F32)
        total = part if total is None else total + part
    return total


def lanes(row):
    total = row[:, :128]
    for start in range(128, row.shape[1], 128):
        total = total + row[:, start : start + 128]
    return total


def cone_project(normal, first, second, friction):
    slide = jnp.sqrt(first * first + second * second)
    inside = slide <= friction * normal
    polar = friction * slide <= -normal
    outside = jnp.logical_not(jnp.logical_or(inside, polar))
    onto = (friction * slide + normal) / (friction * friction + 1.0)
    scale = friction * onto / jnp.where(outside, slide, 1.0)
    scale = jnp.where(inside, 1.0, jnp.where(polar, 0.0, scale))
    new_normal = jnp.where(inside, normal, jnp.where(polar, 0.0, onto))
    return [new_normal, scale * first, scale * second]


def kernel(
    layers,
    cells,
    depth,
    free_hbm,
    mass_hbm,
    jacobian_hbm,
    impulses_hbm,
    previous_hbm,
    compliance_hbm,
    offset_hbm,
    friction_hbm,
    near_hbm,
    far_hbm,
    counts_hbm,
    layer_hbm,
    side_hbm,
    impulses_out,
    velocity_out,
    near_hot,
    near_mask,
    far_hot,
    far_mask,
    halo_hot,
    halo_mask,
    near_jac,
    far_jac,
    side_out,
    side_in,
    sent,
    received,
    sum_out,
    sum_in,
    side_sems,
    phase_send,
    phase_recv,
    sum_send,
    sum_recv,
    free_ref,
    mass_ref,
    jacobian_ref,
    impulses_ref,
    previous_ref,
    compliance_ref,
    offset_ref,
    friction_ref,
    near_ref,
    far_ref,
    counts_ref,
    layer_ref,
    side_ref,
    load_sems,
):
    g = lax.axis_index("gz")
    x = lax.axis_index("xy")
    below, above = (g + layers - 1) % layers, (g + 1) % layers
    lower, higher = (x + cells - 1) % cells, (x + 1) % cells
    line = x // depth * depth
    peers = [
        [
            ((g + step) % layers, (x + depth * stride) % cells)
            for step in range(layers)
            for stride in range(cells // depth)
            if step + stride
        ],
        [(g, line + (x - line + step) % depth) for step in range(1, depth)],
    ]
    around = [
        (g, lower),
        (g, higher),
        (below, x),
        (above, x),
        (below, lower),
        (below, higher),
        (above, lower),
        (above, higher),
    ]

    loads = [
        pltpu.make_async_copy(source, target, load_sems.at[number])
        for number, (source, target) in enumerate(
            (
                (far_hbm, far_ref),
                (near_hbm, near_ref),
                (side_hbm, side_ref),
                (jacobian_hbm, jacobian_ref),
                (impulses_hbm, impulses_ref),
                (previous_hbm, previous_ref),
                (counts_hbm, counts_ref),
                (layer_hbm, layer_ref),
                (free_hbm, free_ref),
                (mass_hbm, mass_ref),
                (compliance_hbm, compliance_ref),
                (offset_hbm, offset_ref),
                (friction_hbm, friction_ref),
            )
        )
    ]
    for load in loads:
        load.start()

    barrier = pltpu.get_barrier_semaphore()
    greeted = around + peers[0] + peers[1]
    for device in greeted:
        pl.semaphore_signal(barrier, inc=1, device_id=device, device_id_type=MESH)

    def remote(src, dst, send_sem, recv_sem, device):
        copy = pltpu.make_async_remote_copy(
            src_ref=src,
            dst_ref=dst,
            send_sem=send_sem,
            recv_sem=recv_sem,
            device_id=device,
            device_id_type=MESH,
        )
        copy.start()

    for load in loads:
        load.wait()
    slabs = near_jac.shape[2] // 128
    near_jac[...] = jnp.zeros_like(near_jac)
    far_jac[...] = jnp.zeros_like(far_jac)
    for r in range(3):
        for t in range(slabs):
            columns = slice(128 * t, 128 * t + 128)
            near_jac[r, 0:6, columns] = jacobian_ref[pl.ds(12 * r * slabs + t, 6, slabs), :]
            far_jac[r, 0:6, columns] = jacobian_ref[pl.ds((12 * r + 6) * slabs + t, 6, slabs), :]
    side_rows = side_ref.shape[1]
    side_list = side_ref[...].astype(F32)
    pad = jnp.full((1, WIDE - side_rows), -1.0, F32)
    side_row = jnp.concatenate([side_list[0:1], pad, side_list[1:2], pad], axis=1)
    side_out[...] = jnp.broadcast_to(side_row, side_out.shape)

    own = free_ref.shape[2]
    layer_rows = layer_ref.shape[1]
    section = own + layer_rows
    far = far_ref[...]
    far = jnp.where(
        far < section, far, jnp.where(far < section + side_rows, far + (3 * WIDE - section), far + (4 * WIDE - section - side_rows))
    )
    set_hot(far, far_hot, far_mask)
    set_hot(near_ref[...], near_hot, near_mask)

    pl.semaphore_wait(barrier, len(greeted))
    remote(side_out, side_in, side_sems.at[0], side_sems.at[1], (above, x))

    slot = lax.broadcasted_iota(jnp.int32, (1, 128), 1)
    counts = counts_ref[...]
    alive = jnp.concatenate(
        [(slot < counts[:, b : b + 1]).astype(F32) for b in range(counts.shape[1])], axis=1
    )
    softness = compliance_ref[...]
    friction = friction_ref[...]
    offset = offset_ref[...]
    sphere_row = lax.broadcasted_iota(jnp.int32, (8, own), 0)
    weights = jnp.where(
        sphere_row < 3, mass_ref[0:1, :], jnp.where(sphere_row < 6, mass_ref[1:2, :], 0.0)
    )
    free = jnp.concatenate([free_ref[j] for j in range(6)] + [jnp.zeros((2, own), F32)], axis=0)

    def set_halo():
        pltpu.make_async_copy(side_in, side_in, side_sems.at[1]).wait()
        layer = layer_ref[...]
        other = side_in[0:1, :].astype(jnp.int32)
        relative = other - own
        row = lax.broadcasted_iota(jnp.int32, (layer_rows, 2 * WIDE), 0)
        hot = (row == relative).astype(F32).astype(BF16)
        parts = jnp.concatenate(
            [jnp.broadcast_to(layer >> 8, (8, layer_rows)), jnp.broadcast_to(layer & 255, (8, layer_rows))], axis=0
        )
        found = jnp.dot(parts.astype(F32).astype(BF16), hot, preferred_element_type=F32)
        composed = (found[0:1] * 256.0 + found[8:9]).astype(jnp.int32)
        composed = jnp.where(relative >= 0, composed, -1)
        mine = side_row.astype(jnp.int32)
        mine = jnp.where(mine < own, mine, -1)
        bottom, first, last = g == 0, x == 0, x == cells - 1
        none = jnp.full((1, WIDE), -1, jnp.int32)
        to_layer = jnp.concatenate([layer, jnp.full((1, WIDE - layer_rows), -1, jnp.int32)], axis=1)
        index = jnp.concatenate(
            [
                jnp.where(bottom, none, to_layer),
                jnp.where(first, none, mine[:, :WIDE]),
                jnp.where(last, none, mine[:, WIDE:]),
                jnp.where(jnp.logical_or(bottom, first), none, composed[:, :WIDE]),
                jnp.where(jnp.logical_or(bottom, last), none, composed[:, WIDE:]),
            ],
            axis=1,
        )
        set_hot(index, halo_hot, halo_mask)

    def part(ref, phase, number):
        return ref.at[phase, :, pl.ds(number * WIDE, WIDE)]

    def arrive(phase):
        pltpu.make_async_copy(received.at[phase], received.at[phase], phase_recv.at[phase]).wait()

    def collect(phase, impulse, between=None):
        far_terms = far_jac[0] * impulse[0] + far_jac[1] * impulse[1] + far_jac[2] * impulse[2]
        far_tiles = scatter(far_terms, far_hot, far_mask)
        for number in range(3):
            sent[phase, :, number * WIDE : (number + 1) * WIDE] = far_tiles[2 + number]
        for number, segment, device in (
            (1, 4, (above, lower)),
            (2, 3, (above, higher)),
            (1, 2, (g, lower)),
            (2, 1, (g, higher)),
            (0, 0, (above, x)),
        ):
            remote(part(sent, phase, number), part(received, phase, segment), phase_send.at[phase], phase_recv.at[phase], device)
        near_terms = near_jac[0] * impulse[0] + near_jac[1] * impulse[1] + near_jac[2] * impulse[2]
        near_tiles = scatter(near_terms, near_hot, near_mask)
        if between is not None:
            between()
        arrive(phase)
        halo_tiles = scatter(received[phase], halo_hot, halo_mask)
        return jnp.concatenate(
            [far_tiles[i] + near_tiles[i] + halo_tiles[i] for i in range(2)], axis=1
        )

    def rows_of(phase, velocity):
        own_tiles = [velocity[:, :WIDE], velocity[:, WIDE:]]
        sent[phase] = gather(own_tiles, range(2), halo_hot, halo_mask)
        for segment, device in (
            (3, (below, lower)),
            (4, (below, higher)),
            (1, (g, lower)),
            (2, (g, higher)),
            (0, (below, x)),
        ):
            remote(part(sent, phase, segment), part(received, phase, segment), phase_send.at[phase], phase_recv.at[phase], device)
        near_rows = gather(own_tiles, range(2), near_hot, near_mask)
        far_rows = gather(own_tiles, range(2), far_hot, far_mask)
        partial = [near_jac[r] * near_rows for r in range(3)]
        arrive(phase)
        segments = [received[phase, :, i * WIDE : (i + 1) * WIDE] for i in range(5)]
        far_rows = far_rows + gather(
            [segments[0], segments[2] + segments[4], segments[1] + segments[3]], (2, 3, 4), far_hot, far_mask
        )
        return [
            jnp.sum(partial[r] + far_jac[r] * far_rows, axis=0, keepdims=True) for r in range(3)
        ]

    def all_sum(iteration, value):
        for number in range(ROUNDS):
            at = iteration * ROUNDS + number
            count = len(peers[number])
            sum_out[at] = value
            for step, device in enumerate(peers[number]):
                remote(sum_out.at[at], sum_in.at[at, step], sum_send.at[at], sum_recv.at[at], device)
            landed = sum_in.at[at, pl.ds(0, count)]
            pltpu.make_async_copy(landed, landed, sum_recv.at[at]).wait()
            terms = [value] + [sum_in[at, step] for step in range(count)]
            while len(terms) > 1:
                pairs = [a + b for a, b in zip(terms[::2], terms[1::2])]
                terms = pairs + terms[2 * len(pairs) :]
            value = terms[0]
        return value

    factors = momentum_factors(ITERS)
    current = [alive * impulses_ref[r] for r in range(3)]
    earlier = [alive * previous_ref[r] for r in range(3)]
    guess = [alive * (current[r] + factors[0] * (current[r] - earlier[r])) for r in range(3)]
    for iteration in range(ITERS):
        phase = 3 * iteration
        velocity = free + weights * collect(phase, guess, set_halo if iteration == 0 else None)
        rows = rows_of(phase + 1, velocity)
        rows[0] = rows[0] + offset
        gradient = [alive * (rows[r] + softness * guess[r]) for r in range(3)]
        squares = gradient[0] * gradient[0] + gradient[1] * gradient[1] + gradient[2] * gradient[2]
        norm = lanes(squares)
        soft = lanes(softness * squares)
        sums = collect(phase + 2, gradient)
        curve = jnp.sum(lanes(weights * sums * sums), axis=0, keepdims=True) + soft
        value = all_sum(iteration, jnp.concatenate([norm, curve], axis=0))
        total = jnp.sum(value, axis=1, keepdims=True)
        step_size = total[0:1] / (total[1:2] + EPSILON)
        moved = [guess[r] - step_size * gradient[r] for r in range(3)]
        updated = [alive * v for v in cone_project(moved[0], moved[1], moved[2], friction)]
        if iteration + 1 < ITERS:
            guess = [
                alive * (updated[r] + factors[iteration + 1] * (updated[r] - current[r]))
                for r in range(3)
            ]
        current = updated
    for r in range(3):
        impulses_out[r] = current[r]
    final = free + weights * collect(PHASES - 1, current)
    for j in range(6):
        velocity_out[j] = final[j : j + 1, :]

    pltpu.make_async_copy(side_out, side_out, side_sems.at[0]).wait()
    for phase in range(PHASES):
        pltpu.make_async_copy(received.at[phase], received.at[phase], phase_send.at[phase]).wait()
    for at in range(ITERS * ROUNDS):
        gone = sum_in.at[at, pl.ds(0, len(peers[at % ROUNDS]))]
        pltpu.make_async_copy(gone, gone, sum_send.at[at]).wait()


def solution(mesh):
    layers, cells = mesh.shape["gz"], mesh.shape["xy"]
    depth = 16

    def on_device(
        velocity_free,
        inverse_mass,
        jacobian,
        impulses,
        previous_impulses,
        compliance,
        offset,
        friction,
        body_near,
        body_far,
        block_counts,
        layer_send,
        side_send,
    ):
        own = velocity_free.shape[3]
        contacts = jacobian.shape[3]
        vmem = pl.BlockSpec(memory_space=pltpu.VMEM)
        sums = ITERS * ROUNDS
        partners = max(layers * (cells // depth), depth) - 1
        operands = (
            velocity_free.reshape(6, 1, own),
            inverse_mass[0, 0],
            jacobian.reshape(36 * contacts // 128, 128),
            impulses.reshape(3, 1, contacts),
            previous_impulses.reshape(3, 1, contacts),
            compliance[0],
            offset[0],
            friction[0],
            body_near[0],
            body_far[0],
            block_counts[0],
            layer_send[0],
            side_send[0, 0],
        )
        outs = pl.pallas_call(
            functools.partial(kernel, layers, cells, depth),
            out_shape=(
                jax.ShapeDtypeStruct((3, 1, contacts), F32),
                jax.ShapeDtypeStruct((6, 1, own), F32),
            ),
            in_specs=[pl.BlockSpec(memory_space=pl.ANY)] * 13,
            out_specs=(vmem, vmem),
            scratch_shapes=[
                pltpu.VMEM((WIDE, contacts), BF16),
                pltpu.VMEM((2, 16, contacts), BF16),
                pltpu.VMEM((WIDE, contacts), BF16),
                pltpu.VMEM((5, 16, contacts), BF16),
                pltpu.VMEM((WIDE, 5 * WIDE), BF16),
                pltpu.VMEM((2, 16, 5 * WIDE), BF16),
                pltpu.VMEM((3, 8, contacts), F32),
                pltpu.VMEM((3, 8, contacts), F32),
                pltpu.VMEM((8, 2 * WIDE), F32),
                pltpu.VMEM((8, 2 * WIDE), F32),
                pltpu.VMEM((PHASES, 8, 5 * WIDE), F32),
                pltpu.VMEM((PHASES, 8, 5 * WIDE), F32),
                pltpu.VMEM((sums, 2, 128), F32),
                pltpu.VMEM((sums, partners, 2, 128), F32),
                pltpu.SemaphoreType.DMA((2,)),
                pltpu.SemaphoreType.DMA((PHASES,)),
                pltpu.SemaphoreType.DMA((PHASES,)),
                pltpu.SemaphoreType.DMA((sums,)),
                pltpu.SemaphoreType.DMA((sums,)),
                *[pltpu.VMEM(v.shape, v.dtype) for v in operands],
                pltpu.SemaphoreType.DMA((len(operands),)),
            ],
            compiler_params=pltpu.CompilerParams(
                collective_id=0, has_side_effects=True, vmem_limit_bytes=56 << 20
            ),
        )(*operands)
        return outs[0].reshape(1, 1, 3, contacts), outs[1].reshape(1, 1, 6, own)

    field = P("gz", "xy", None, None)
    line = P("gz", "xy", None)
    return jax.shard_map(
        on_device,
        mesh=mesh,
        in_specs=(field,) * 5 + (line,) * 7 + (field,),
        out_specs=(field, field),
        check_vma=False,
    )
```

```python
import functools
import math

import jax
import jax.numpy as jnp
from jax import lax
from jax.experimental import pallas as pl
from jax.experimental.pallas import tpu as pltpu
from jax.sharding import PartitionSpec as P

ITERS = 2
EPSILON = 1e-06
THETA_START = 0.3

MESH = pl.DeviceIdType.MESH
F32 = jnp.float32
BF16 = jnp.bfloat16
WIDE = 256
PHASES = 3 * ITERS + 1
SPREADS = tuple(3 * iteration + 1 for iteration in range(ITERS))
ROUNDS = 2


def theta_after(theta_value):
    return 0.5 * (
        -theta_value * theta_value + theta_value * math.sqrt(theta_value * theta_value + 4.0)
    )


def momentum_factors(iteration_count):
    thetas = [THETA_START]
    for iteration in range(iteration_count):
        thetas.append(theta_after(thetas[-1]))
    return [
        thetas[position]
        * (1.0 - thetas[position])
        / (thetas[position] * thetas[position] + thetas[position + 1])
        for position in range(iteration_count)
    ]


def halves(rows):
    high = rows.astype(BF16).astype(F32)
    return jnp.concatenate([high, rows - high], axis=0).astype(BF16)


def set_hot(index, hot_ref, mask_ref):
    lane = jnp.where(index < 0, -1, index & (WIDE - 1))
    tile = index >> 8
    width = index.shape[1]
    for start in range(0, width, WIDE):
        part = lane[:, start : start + WIDE]
        row = lax.broadcasted_iota(jnp.int32, (WIDE, WIDE), 0)
        hot_ref[:, start : start + WIDE] = (row == part).astype(F32).astype(BF16)
    for number in range(mask_ref.shape[0]):
        mask = (tile == number).astype(F32)
        mask_ref[number] = jnp.broadcast_to(mask, (16, width)).astype(BF16)


def scatter(rows, hot_ref, mask_ref):
    both = halves(rows)
    tiles = mask_ref.shape[0]
    left = jnp.concatenate([both * mask_ref[number] for number in range(tiles)], axis=0)
    sums = lax.dot_general(
        left, hot_ref[...], (((1,), (1,)), ((), ())), preferred_element_type=F32
    )
    return [
        sums[16 * number : 16 * number + 8] + sums[16 * number + 8 : 16 * number + 16]
        for number in range(tiles)
    ]


def gather(tiles, numbers, hot_ref, mask_ref):
    left = jnp.concatenate([halves(tile) for tile in tiles], axis=0)
    found = jnp.dot(left, hot_ref[...], preferred_element_type=F32)
    total = None
    for position, number in enumerate(numbers):
        part = found[16 * position : 16 * position + 8] + found[16 * position + 8 : 16 * position + 16]
        part = part * mask_ref[number][:8].astype(F32)
        total = part if total is None else total + part
    return total


def lanes(row):
    total = row[:, :128]
    for start in range(128, row.shape[1], 128):
        total = total + row[:, start : start + 128]
    return total


def cone_project(normal, first, second, friction):
    slide = jnp.sqrt(first * first + second * second)
    inside = slide <= friction * normal
    polar = friction * slide <= -normal
    outside = jnp.logical_not(jnp.logical_or(inside, polar))
    onto = (friction * slide + normal) / (friction * friction + 1.0)
    scale = friction * onto / jnp.where(outside, slide, 1.0)
    scale = jnp.where(inside, 1.0, jnp.where(polar, 0.0, scale))
    new_normal = jnp.where(inside, normal, jnp.where(polar, 0.0, onto))
    return [new_normal, scale * first, scale * second]


def kernel(
    layers,
    cells,
    depth,
    free_hbm,
    mass_hbm,
    jacobian_hbm,
    impulses_hbm,
    previous_hbm,
    compliance_hbm,
    offset_hbm,
    friction_hbm,
    near_hbm,
    far_hbm,
    counts_hbm,
    layer_hbm,
    side_hbm,
    impulses_out,
    velocity_out,
    near_hot,
    near_mask,
    far_hot,
    far_mask,
    halo_hot,
    halo_mask,
    near_jac,
    far_jac,
    side_out,
    side_in,
    sent,
    received,
    sum_out,
    sum_in,
    side_sems,
    phase_send,
    phase_recv,
    sum_send,
    sum_recv,
    token_sems,
    free_ref,
    mass_ref,
    jacobian_ref,
    impulses_ref,
    previous_ref,
    compliance_ref,
    offset_ref,
    friction_ref,
    near_ref,
    far_ref,
    counts_ref,
    layer_ref,
    side_ref,
    load_sems,
):
    g = lax.axis_index("gz")
    x = lax.axis_index("xy")
    has_below, has_above = g > 0, g < layers - 1
    has_lower, has_higher = x > 0, x < cells - 1
    beside = has_lower.astype(jnp.int32) + has_higher.astype(jnp.int32)
    upward = beside + jnp.where(has_above, beside + 1, 0)
    downward = beside + jnp.where(has_below, beside + 1, 0)
    below, above = (g + layers - 1) % layers, (g + 1) % layers
    lower, higher = (x + cells - 1) % cells, (x + 1) % cells
    line = x // depth * depth
    peers = [
        [
            ((g + step) % layers, (x + depth * stride) % cells)
            for step in range(layers)
            for stride in range(cells // depth)
            if step + stride
        ],
        [(g, line + (x - line + step) % depth) for step in range(1, depth)],
    ]
    around = [
        (g, lower),
        (g, higher),
        (below, x),
        (above, x),
        (below, lower),
        (below, higher),
        (above, lower),
        (above, higher),
    ]

    loads = [
        pltpu.make_async_copy(source, target, load_sems.at[number])
        for number, (source, target) in enumerate(
            (
                (far_hbm, far_ref),
                (near_hbm, near_ref),
                (side_hbm, side_ref),
                (jacobian_hbm, jacobian_ref),
                (impulses_hbm, impulses_ref),
                (previous_hbm, previous_ref),
                (counts_hbm, counts_ref),
                (layer_hbm, layer_ref),
                (free_hbm, free_ref),
                (mass_hbm, mass_ref),
                (compliance_hbm, compliance_ref),
                (offset_hbm, offset_ref),
                (friction_hbm, friction_ref),
            )
        )
    ]
    for load in loads:
        load.start()

    received[...] = jnp.zeros_like(received)
    side_in[...] = jnp.full_like(side_in, -1.0)

    barrier = pltpu.get_barrier_semaphore()
    def along(step):
        return (g, line + (x - line + step) % depth)

    greeted = around + peers[0] + [along(step) for step in (1, 2, depth - 1, depth - 2)]
    for device in greeted:
        pl.semaphore_signal(barrier, inc=1, device_id=device, device_id_type=MESH)

    def remote(src, dst, send_sem, recv_sem, device):
        copy = pltpu.make_async_remote_copy(
            src_ref=src,
            dst_ref=dst,
            send_sem=send_sem,
            recv_sem=recv_sem,
            device_id=device,
            device_id_type=MESH,
        )
        copy.start()

    for load in loads:
        load.wait()
    slabs = near_jac.shape[2] // 128
    near_jac[...] = jnp.zeros_like(near_jac)
    far_jac[...] = jnp.zeros_like(far_jac)
    for r in range(3):
        for t in range(slabs):
            columns = slice(128 * t, 128 * t + 128)
            near_jac[r, 0:6, columns] = jacobian_ref[pl.ds(12 * r * slabs + t, 6, slabs), :]
            far_jac[r, 0:6, columns] = jacobian_ref[pl.ds((12 * r + 6) * slabs + t, 6, slabs), :]
    side_rows = side_ref.shape[1]
    side_list = side_ref[...].astype(F32)
    pad = jnp.full((1, WIDE - side_rows), -1.0, F32)
    side_row = jnp.concatenate([side_list[0:1], pad, side_list[1:2], pad], axis=1)
    side_out[...] = jnp.broadcast_to(side_row, side_out.shape)

    own = free_ref.shape[2]
    layer_rows = layer_ref.shape[1]
    section = own + layer_rows
    far = far_ref[...]
    far = jnp.where(
        far < section, far, jnp.where(far < section + side_rows, far + (3 * WIDE - section), far + (4 * WIDE - section - side_rows))
    )
    set_hot(far, far_hot, far_mask)
    set_hot(near_ref[...], near_hot, near_mask)

    pl.semaphore_wait(barrier, len(greeted))
    @pl.when(has_above)
    def _():
        remote(side_out, side_in, side_sems.at[0], side_sems.at[1], (above, x))

    slot = lax.broadcasted_iota(jnp.int32, (1, 128), 1)
    counts = counts_ref[...]
    alive = jnp.concatenate(
        [(slot < counts[:, b : b + 1]).astype(F32) for b in range(counts.shape[1])], axis=1
    )
    softness = compliance_ref[...]
    friction = friction_ref[...]
    offset = offset_ref[...]
    sphere_row = lax.broadcasted_iota(jnp.int32, (8, own), 0)
    weights = jnp.where(
        sphere_row < 3, mass_ref[0:1, :], jnp.where(sphere_row < 6, mass_ref[1:2, :], 0.0)
    )
    free = jnp.concatenate([free_ref[j] for j in range(6)] + [jnp.zeros((2, own), F32)], axis=0)

    def set_halo():
        @pl.when(has_below)
        def _():
            pltpu.make_async_copy(side_in, side_in, side_sems.at[1]).wait()

        layer = layer_ref[...]
        other = side_in[0:1, :].astype(jnp.int32)
        relative = other - own
        row = lax.broadcasted_iota(jnp.int32, (layer_rows, 2 * WIDE), 0)
        hot = (row == relative).astype(F32).astype(BF16)
        parts = jnp.concatenate(
            [jnp.broadcast_to(layer >> 8, (8, layer_rows)), jnp.broadcast_to(layer & 255, (8, layer_rows))], axis=0
        )
        found = jnp.dot(parts.astype(F32).astype(BF16), hot, preferred_element_type=F32)
        composed = (found[0:1] * 256.0 + found[8:9]).astype(jnp.int32)
        composed = jnp.where(relative >= 0, composed, -1)
        mine = side_row.astype(jnp.int32)
        mine = jnp.where(mine < own, mine, -1)
        bottom, first, last = g == 0, x == 0, x == cells - 1
        none = jnp.full((1, WIDE), -1, jnp.int32)
        to_layer = jnp.concatenate([layer, jnp.full((1, WIDE - layer_rows), -1, jnp.int32)], axis=1)
        index = jnp.concatenate(
            [
                jnp.where(bottom, none, to_layer),
                jnp.where(first, none, mine[:, :WIDE]),
                jnp.where(last, none, mine[:, WIDE:]),
                jnp.where(jnp.logical_or(bottom, first), none, composed[:, :WIDE]),
                jnp.where(jnp.logical_or(bottom, last), none, composed[:, WIDE:]),
            ],
            axis=1,
        )
        set_hot(index, halo_hot, halo_mask)

    def part(ref, phase, number):
        return ref.at[phase, :, pl.ds(number * WIDE, WIDE)]

    def pass_token(number):
        for step in (2 << number, depth - (2 << number)):
            pl.semaphore_signal(
                token_sems.at[number], inc=1, device_id=along(step), device_id_type=MESH
            )

    def send(phase, number, segment, device, valid):
        @pl.when(valid)
        def _():
            remote(
                part(sent, phase, number),
                part(received, phase, segment),
                phase_send.at[phase],
                phase_recv.at[phase],
                device,
            )

    def await_segments(phase, sem, count):
        for number in (1, 2, 3, 5):

            @pl.when(count == number)
            def _():
                moved = received.at[phase, :, pl.ds(0, number * WIDE)]
                pltpu.make_async_copy(moved, moved, sem.at[phase]).wait()

    def collect(phase, impulse, between=None):
        far_terms = far_jac[0] * impulse[0] + far_jac[1] * impulse[1] + far_jac[2] * impulse[2]
        far_tiles = scatter(far_terms, far_hot, far_mask)
        for number in range(3):
            sent[phase, :, number * WIDE : (number + 1) * WIDE] = far_tiles[2 + number]
        send(phase, 1, 4, (above, lower), jnp.logical_and(has_above, has_lower))
        send(phase, 2, 3, (above, higher), jnp.logical_and(has_above, has_higher))
        send(phase, 1, 2, (g, lower), has_lower)
        send(phase, 2, 1, (g, higher), has_higher)
        send(phase, 0, 0, (above, x), has_above)
        near_terms = near_jac[0] * impulse[0] + near_jac[1] * impulse[1] + near_jac[2] * impulse[2]
        near_tiles = scatter(near_terms, near_hot, near_mask)
        if between is not None:
            between()
        await_segments(phase, phase_recv, downward)
        halo_tiles = scatter(received[phase], halo_hot, halo_mask)
        return jnp.concatenate(
            [far_tiles[i] + near_tiles[i] + halo_tiles[i] for i in range(2)], axis=1
        )

    def rows_of(phase, velocity):
        own_tiles = [velocity[:, :WIDE], velocity[:, WIDE:]]
        sent[phase] = gather(own_tiles, range(2), halo_hot, halo_mask)
        send(phase, 3, 3, (below, lower), jnp.logical_and(has_below, has_lower))
        send(phase, 4, 4, (below, higher), jnp.logical_and(has_below, has_higher))
        send(phase, 1, 1, (g, lower), has_lower)
        send(phase, 2, 2, (g, higher), has_higher)
        send(phase, 0, 0, (below, x), has_below)
        near_rows = gather(own_tiles, range(2), near_hot, near_mask)
        far_rows = gather(own_tiles, range(2), far_hot, far_mask)
        partial = [near_jac[r] * near_rows for r in range(3)]
        await_segments(phase, phase_recv, upward)
        segments = [received[phase, :, i * WIDE : (i + 1) * WIDE] for i in range(5)]
        far_rows = far_rows + gather(
            [segments[0], segments[2] + segments[4], segments[1] + segments[3]], (2, 3, 4), far_hot, far_mask
        )
        return [
            jnp.sum(partial[r] + far_jac[r] * far_rows, axis=0, keepdims=True) for r in range(3)
        ]

    def all_sum(iteration, value):
        for number in range(ROUNDS):
            at = iteration * ROUNDS + number
            count = len(peers[number])
            sum_out[at] = value
            for step, device in enumerate(peers[number]):
                remote(sum_out.at[at], sum_in.at[at, step], sum_send.at[at], sum_recv.at[at], device)
            landed = sum_in.at[at, pl.ds(0, count)]
            pltpu.make_async_copy(landed, landed, sum_recv.at[at]).wait()
            terms = [value] + [sum_in[at, step] for step in range(count)]
            while len(terms) > 1:
                pairs = [a + b for a, b in zip(terms[::2], terms[1::2])]
                terms = pairs + terms[2 * len(pairs) :]
            value = terms[0]
        return value

    pass_token(0)
    factors = momentum_factors(ITERS)
    current = [alive * impulses_ref[r] for r in range(3)]
    earlier = [alive * previous_ref[r] for r in range(3)]
    guess = [alive * (current[r] + factors[0] * (current[r] - earlier[r])) for r in range(3)]
    for iteration in range(ITERS):
        phase = 3 * iteration
        velocity = free + weights * collect(phase, guess, set_halo if iteration == 0 else None)
        if iteration == 0:
            pl.semaphore_wait(token_sems.at[0], 2)
            pass_token(1)
        rows = rows_of(phase + 1, velocity)
        rows[0] = rows[0] + offset
        gradient = [alive * (rows[r] + softness * guess[r]) for r in range(3)]
        squares = gradient[0] * gradient[0] + gradient[1] * gradient[1] + gradient[2] * gradient[2]
        norm = lanes(squares)
        soft = lanes(softness * squares)
        sums = collect(phase + 2, gradient)
        if iteration == 0:
            pl.semaphore_wait(token_sems.at[1], 2)
        curve = jnp.sum(lanes(weights * sums * sums), axis=0, keepdims=True) + soft
        value = all_sum(iteration, jnp.concatenate([norm, curve], axis=0))
        total = jnp.sum(value, axis=1, keepdims=True)
        step_size = total[0:1] / (total[1:2] + EPSILON)
        moved = [guess[r] - step_size * gradient[r] for r in range(3)]
        updated = [alive * v for v in cone_project(moved[0], moved[1], moved[2], friction)]
        if iteration + 1 < ITERS:
            guess = [
                alive * (updated[r] + factors[iteration + 1] * (updated[r] - current[r]))
                for r in range(3)
            ]
        current = updated
    for r in range(3):
        impulses_out[r] = current[r]
    final = free + weights * collect(PHASES - 1, current)
    for j in range(6):
        velocity_out[j] = final[j : j + 1, :]

    @pl.when(has_above)
    def _():
        pltpu.make_async_copy(side_out, side_out, side_sems.at[0]).wait()

    for phase in range(PHASES):
        await_segments(phase, phase_send, downward if phase in SPREADS else upward)
    for at in range(ITERS * ROUNDS):
        gone = sum_in.at[at, pl.ds(0, len(peers[at % ROUNDS]))]
        pltpu.make_async_copy(gone, gone, sum_send.at[at]).wait()


def solution(mesh):
    layers, cells = mesh.shape["gz"], mesh.shape["xy"]
    depth = 16

    def on_device(
        velocity_free,
        inverse_mass,
        jacobian,
        impulses,
        previous_impulses,
        compliance,
        offset,
        friction,
        body_near,
        body_far,
        block_counts,
        layer_send,
        side_send,
    ):
        own = velocity_free.shape[3]
        contacts = jacobian.shape[3]
        vmem = pl.BlockSpec(memory_space=pltpu.VMEM)
        sums = ITERS * ROUNDS
        partners = max(layers * (cells // depth), depth) - 1
        operands = (
            velocity_free.reshape(6, 1, own),
            inverse_mass[0, 0],
            jacobian.reshape(36 * contacts // 128, 128),
            impulses.reshape(3, 1, contacts),
            previous_impulses.reshape(3, 1, contacts),
            compliance[0],
            offset[0],
            friction[0],
            body_near[0],
            body_far[0],
            block_counts[0],
            layer_send[0],
            side_send[0, 0],
        )
        outs = pl.pallas_call(
            functools.partial(kernel, layers, cells, depth),
            out_shape=(
                jax.ShapeDtypeStruct((3, 1, contacts), F32),
                jax.ShapeDtypeStruct((6, 1, own), F32),
            ),
            in_specs=[pl.BlockSpec(memory_space=pl.ANY)] * 13,
            out_specs=(vmem, vmem),
            scratch_shapes=[
                pltpu.VMEM((WIDE, contacts), BF16),
                pltpu.VMEM((2, 16, contacts), BF16),
                pltpu.VMEM((WIDE, contacts), BF16),
                pltpu.VMEM((5, 16, contacts), BF16),
                pltpu.VMEM((WIDE, 5 * WIDE), BF16),
                pltpu.VMEM((2, 16, 5 * WIDE), BF16),
                pltpu.VMEM((3, 8, contacts), F32),
                pltpu.VMEM((3, 8, contacts), F32),
                pltpu.VMEM((8, 2 * WIDE), F32),
                pltpu.VMEM((8, 2 * WIDE), F32),
                pltpu.VMEM((PHASES, 8, 5 * WIDE), F32),
                pltpu.VMEM((PHASES, 8, 5 * WIDE), F32),
                pltpu.VMEM((sums, 2, 128), F32),
                pltpu.VMEM((sums, partners, 2, 128), F32),
                pltpu.SemaphoreType.DMA((2,)),
                pltpu.SemaphoreType.DMA((PHASES,)),
                pltpu.SemaphoreType.DMA((PHASES,)),
                pltpu.SemaphoreType.DMA((sums,)),
                pltpu.SemaphoreType.DMA((sums,)),
                pltpu.SemaphoreType.REGULAR((2,)),
                *[pltpu.VMEM(v.shape, v.dtype) for v in operands],
                pltpu.SemaphoreType.DMA((len(operands),)),
            ],
            compiler_params=pltpu.CompilerParams(
                collective_id=0, has_side_effects=True, vmem_limit_bytes=56 << 20
            ),
        )(*operands)
        return outs[0].reshape(1, 1, 3, contacts), outs[1].reshape(1, 1, 6, own)

    field = P("gz", "xy", None, None)
    line = P("gz", "xy", None)
    return jax.shard_map(
        on_device,
        mesh=mesh,
        in_specs=(field,) * 5 + (line,) * 7 + (field,),
        out_specs=(field, field),
        check_vma=False,
    )
```

```python
import functools
import math

import jax
import jax.numpy as jnp
from jax import lax
from jax.experimental import pallas as pl
from jax.experimental.pallas import tpu as pltpu
from jax.sharding import PartitionSpec as P

ITERS = 2
EPSILON = 1e-06
THETA_START = 0.3

MESH = pl.DeviceIdType.MESH
F32 = jnp.float32
BF16 = jnp.bfloat16
WIDE = 256
PHASES = 3 * ITERS + 1
SPREADS = tuple(3 * iteration + 1 for iteration in range(ITERS))
ROUNDS = 2


def theta_after(theta_value):
    return 0.5 * (
        -theta_value * theta_value + theta_value * math.sqrt(theta_value * theta_value + 4.0)
    )


def momentum_factors(iteration_count):
    thetas = [THETA_START]
    for iteration in range(iteration_count):
        thetas.append(theta_after(thetas[-1]))
    return [
        thetas[position]
        * (1.0 - thetas[position])
        / (thetas[position] * thetas[position] + thetas[position + 1])
        for position in range(iteration_count)
    ]


def halves(rows):
    high = rows.astype(BF16).astype(F32)
    return jnp.concatenate([high, rows - high], axis=0).astype(BF16)


def set_hot(index, hot_ref, mask_ref):
    lane = jnp.where(index < 0, -1, index & (WIDE - 1))
    tile = index >> 8
    width = index.shape[1]
    for start in range(0, width, WIDE):
        part = lane[:, start : start + WIDE]
        row = lax.broadcasted_iota(jnp.int32, (WIDE, WIDE), 0)
        hot_ref[:, start : start + WIDE] = (row == part).astype(F32).astype(BF16)
    for number in range(mask_ref.shape[0]):
        mask = (tile == number).astype(F32)
        mask_ref[number] = jnp.broadcast_to(mask, (16, width)).astype(BF16)


def scatter(both, numbers, hot_ref, mask_ref):
    left = jnp.concatenate([both * mask_ref[number] for number in numbers], axis=0)
    sums = lax.dot_general(
        left, hot_ref[...], (((1,), (1,)), ((), ())), preferred_element_type=F32
    )
    return [
        sums[16 * i : 16 * i + 8] + sums[16 * i + 8 : 16 * i + 16]
        for i in range(len(numbers))
    ]


def gather(tiles, numbers, hot_ref, mask_ref):
    left = jnp.concatenate([halves(tile) for tile in tiles], axis=0)
    found = jnp.dot(left, hot_ref[...], preferred_element_type=F32)
    total = None
    for position, number in enumerate(numbers):
        part = found[16 * position : 16 * position + 8] + found[16 * position + 8 : 16 * position + 16]
        part = part * mask_ref[number][:8].astype(F32)
        total = part if total is None else total + part
    return total


def lanes(row):
    total = row[:, :128]
    for start in range(128, row.shape[1], 128):
        total = total + row[:, start : start + 128]
    return total


def cone_project(normal, first, second, friction):
    slide = jnp.sqrt(first * first + second * second)
    inside = slide <= friction * normal
    polar = friction * slide <= -normal
    outside = jnp.logical_not(jnp.logical_or(inside, polar))
    onto = (friction * slide + normal) / (friction * friction + 1.0)
    scale = friction * onto / jnp.where(outside, slide, 1.0)
    scale = jnp.where(inside, 1.0, jnp.where(polar, 0.0, scale))
    new_normal = jnp.where(inside, normal, jnp.where(polar, 0.0, onto))
    return [new_normal, scale * first, scale * second]


def kernel(
    layers,
    cells,
    depth,
    free_hbm,
    mass_hbm,
    jacobian_hbm,
    impulses_hbm,
    previous_hbm,
    compliance_hbm,
    offset_hbm,
    friction_hbm,
    near_hbm,
    far_hbm,
    counts_hbm,
    layer_hbm,
    side_hbm,
    impulses_out,
    velocity_out,
    near_hot,
    near_mask,
    far_hot,
    far_mask,
    halo_hot,
    halo_mask,
    near_jac,
    far_jac,
    side_out,
    side_in,
    sent,
    received,
    sum_out,
    sum_in,
    side_sems,
    phase_send,
    phase_recv,
    sum_send,
    sum_recv,
    token_sems,
    free_ref,
    mass_ref,
    jacobian_ref,
    impulses_ref,
    previous_ref,
    compliance_ref,
    offset_ref,
    friction_ref,
    near_ref,
    far_ref,
    counts_ref,
    layer_ref,
    side_ref,
    load_sems,
):
    g = lax.axis_index("gz")
    x = lax.axis_index("xy")
    has_below, has_above = g > 0, g < layers - 1
    has_lower, has_higher = x > 0, x < cells - 1
    beside = has_lower.astype(jnp.int32) + has_higher.astype(jnp.int32)
    upward = beside + jnp.where(has_above, beside + 1, 0)
    downward = beside + jnp.where(has_below, beside + 1, 0)
    below, above = (g + layers - 1) % layers, (g + 1) % layers
    lower, higher = (x + cells - 1) % cells, (x + 1) % cells
    line = x // depth * depth
    peers = [
        [
            ((g + step) % layers, (x + depth * stride) % cells)
            for step in sorted(range(layers), key=lambda step: -min(step, layers - step))
            for stride in (2, 1, 3, 0)
            if step + stride
        ],
        [(g, line + (x - line + step) % depth) for step in sorted(range(1, depth), key=lambda step: -min(step, depth - step))],
    ]
    around = [
        (g, lower),
        (g, higher),
        (below, x),
        (above, x),
        (below, lower),
        (below, higher),
        (above, lower),
        (above, higher),
    ]

    loads = [
        pltpu.make_async_copy(source, target, load_sems.at[number])
        for number, (source, target) in enumerate(
            (
                (far_hbm, far_ref),
                (near_hbm, near_ref),
                (side_hbm, side_ref),
                (jacobian_hbm, jacobian_ref),
                (impulses_hbm, impulses_ref),
                (previous_hbm, previous_ref),
                (counts_hbm, counts_ref),
                (layer_hbm, layer_ref),
                (free_hbm, free_ref),
                (mass_hbm, mass_ref),
                (compliance_hbm, compliance_ref),
                (offset_hbm, offset_ref),
                (friction_hbm, friction_ref),
            )
        )
    ]
    for load in loads:
        load.start()

    received[...] = jnp.zeros_like(received)
    side_in[...] = jnp.full_like(side_in, -1.0)

    barrier = pltpu.get_barrier_semaphore()
    def along(step):
        return (g, line + (x - line + step) % depth)

    def across(step):
        return (g, (x + depth * step) % cells)

    def through(step):
        return ((g + step) % layers, x)

    both_ways = lambda place, *steps: [place(step) for near in steps for step in (near, -near)]
    greeted = around + both_ways(through, 2) + both_ways(across, 1) + both_ways(along, 1, 2)
    tokens = [
        both_ways(through, 2) + both_ways(across, 1) + both_ways(along, 2),
        both_ways(across, 1) + [across(2)] + both_ways(along, 4),
    ]
    for device in greeted:
        pl.semaphore_signal(barrier, inc=1, device_id=device, device_id_type=MESH)

    def remote(src, dst, send_sem, recv_sem, device):
        copy = pltpu.make_async_remote_copy(
            src_ref=src,
            dst_ref=dst,
            send_sem=send_sem,
            recv_sem=recv_sem,
            device_id=device,
            device_id_type=MESH,
        )
        copy.start()

    for load in loads:
        load.wait()
    slabs = near_jac.shape[2] // 128
    near_jac[...] = jnp.zeros_like(near_jac)
    far_jac[...] = jnp.zeros_like(far_jac)
    for r in range(3):
        for t in range(slabs):
            columns = slice(128 * t, 128 * t + 128)
            near_jac[r, 0:6, columns] = jacobian_ref[pl.ds(12 * r * slabs + t, 6, slabs), :]
            far_jac[r, 0:6, columns] = jacobian_ref[pl.ds((12 * r + 6) * slabs + t, 6, slabs), :]
    side_rows = side_ref.shape[1]
    side_list = side_ref[...].astype(F32)
    pad = jnp.full((1, WIDE - side_rows), -1.0, F32)
    side_row = jnp.concatenate([side_list[0:1], pad, side_list[1:2], pad], axis=1)
    side_out[...] = jnp.broadcast_to(side_row, side_out.shape)

    own = free_ref.shape[2]
    layer_rows = layer_ref.shape[1]
    section = own + layer_rows
    far = far_ref[...]
    far = jnp.where(
        far < section, far, jnp.where(far < section + side_rows, far + (3 * WIDE - section), far + (4 * WIDE - section - side_rows))
    )
    set_hot(far, far_hot, far_mask)
    set_hot(near_ref[...], near_hot, near_mask)

    pl.semaphore_wait(barrier, len(greeted))
    @pl.when(has_above)
    def _():
        remote(side_out, side_in, side_sems.at[0], side_sems.at[1], (above, x))

    slot = lax.broadcasted_iota(jnp.int32, (1, 128), 1)
    counts = counts_ref[...]
    alive = jnp.concatenate(
        [(slot < counts[:, b : b + 1]).astype(F32) for b in range(counts.shape[1])], axis=1
    )
    softness = compliance_ref[...]
    friction = friction_ref[...]
    offset = offset_ref[...]
    sphere_row = lax.broadcasted_iota(jnp.int32, (8, own), 0)
    weights = jnp.where(
        sphere_row < 3, mass_ref[0:1, :], jnp.where(sphere_row < 6, mass_ref[1:2, :], 0.0)
    )
    free = jnp.concatenate([free_ref[j] for j in range(6)] + [jnp.zeros((2, own), F32)], axis=0)

    def set_halo():
        @pl.when(has_below)
        def _():
            pltpu.make_async_copy(side_in, side_in, side_sems.at[1]).wait()

        layer = layer_ref[...]
        other = side_in[0:1, :].astype(jnp.int32)
        relative = other - own
        row = lax.broadcasted_iota(jnp.int32, (layer_rows, 2 * WIDE), 0)
        hot = (row == relative).astype(F32).astype(BF16)
        parts = jnp.concatenate(
            [jnp.broadcast_to(layer >> 8, (8, layer_rows)), jnp.broadcast_to(layer & 255, (8, layer_rows))], axis=0
        )
        found = jnp.dot(parts.astype(F32).astype(BF16), hot, preferred_element_type=F32)
        composed = (found[0:1] * 256.0 + found[8:9]).astype(jnp.int32)
        composed = jnp.where(relative >= 0, composed, -1)
        mine = side_row.astype(jnp.int32)
        mine = jnp.where(mine < own, mine, -1)
        bottom, first, last = g == 0, x == 0, x == cells - 1
        none = jnp.full((1, WIDE), -1, jnp.int32)
        to_layer = jnp.concatenate([layer, jnp.full((1, WIDE - layer_rows), -1, jnp.int32)], axis=1)
        index = jnp.concatenate(
            [
                jnp.where(bottom, none, to_layer),
                jnp.where(first, none, mine[:, :WIDE]),
                jnp.where(last, none, mine[:, WIDE:]),
                jnp.where(jnp.logical_or(bottom, first), none, composed[:, :WIDE]),
                jnp.where(jnp.logical_or(bottom, last), none, composed[:, WIDE:]),
            ],
            axis=1,
        )
        set_hot(index, halo_hot, halo_mask)

    def part(ref, phase, number):
        return ref.at[phase, :, pl.ds(number * WIDE, WIDE)]

    def pass_token(number):
        for device in tokens[number]:
            pl.semaphore_signal(token_sems.at[number], inc=1, device_id=device, device_id_type=MESH)

    def send(phase, number, segment, device, valid):
        @pl.when(valid)
        def _():
            remote(
                part(sent, phase, number),
                part(received, phase, segment),
                phase_send.at[phase],
                phase_recv.at[phase],
                device,
            )

    def await_segments(phase, sem, count):
        for number in (1, 2, 3, 5):

            @pl.when(count == number)
            def _():
                moved = received.at[phase, :, pl.ds(0, number * WIDE)]
                pltpu.make_async_copy(moved, moved, sem.at[phase]).wait()

    def collect(phase, impulse, between=None):
        far_terms = far_jac[0] * impulse[0] + far_jac[1] * impulse[1] + far_jac[2] * impulse[2]
        far_terms = halves(far_terms)
        leaving = scatter(far_terms, (2, 3, 4), far_hot, far_mask)
        for number in range(3):
            sent[phase, :, number * WIDE : (number + 1) * WIDE] = leaving[number]
        send(phase, 1, 4, (above, lower), jnp.logical_and(has_above, has_lower))
        send(phase, 2, 3, (above, higher), jnp.logical_and(has_above, has_higher))
        send(phase, 1, 2, (g, lower), has_lower)
        send(phase, 2, 1, (g, higher), has_higher)
        send(phase, 0, 0, (above, x), has_above)
        near_terms = near_jac[0] * impulse[0] + near_jac[1] * impulse[1] + near_jac[2] * impulse[2]
        near_tiles = scatter(halves(near_terms), (0, 1), near_hot, near_mask)
        far_tiles = scatter(far_terms, (0, 1), far_hot, far_mask)
        if between is not None:
            between()
        await_segments(phase, phase_recv, downward)
        halo_tiles = scatter(halves(received[phase]), (0, 1), halo_hot, halo_mask)
        return jnp.concatenate(
            [far_tiles[i] + near_tiles[i] + halo_tiles[i] for i in range(2)], axis=1
        )

    def rows_of(phase, velocity):
        own_tiles = [velocity[:, :WIDE], velocity[:, WIDE:]]
        sent[phase] = gather(own_tiles, range(2), halo_hot, halo_mask)
        send(phase, 3, 3, (below, lower), jnp.logical_and(has_below, has_lower))
        send(phase, 4, 4, (below, higher), jnp.logical_and(has_below, has_higher))
        send(phase, 1, 1, (g, lower), has_lower)
        send(phase, 2, 2, (g, higher), has_higher)
        send(phase, 0, 0, (below, x), has_below)
        near_rows = gather(own_tiles, range(2), near_hot, near_mask)
        far_rows = gather(own_tiles, range(2), far_hot, far_mask)
        partial = [near_jac[r] * near_rows for r in range(3)]
        await_segments(phase, phase_recv, upward)
        segments = [received[phase, :, i * WIDE : (i + 1) * WIDE] for i in range(5)]
        far_rows = far_rows + gather(
            [segments[0], segments[2] + segments[4], segments[1] + segments[3]], (2, 3, 4), far_hot, far_mask
        )
        return [
            jnp.sum(partial[r] + far_jac[r] * far_rows, axis=0, keepdims=True) for r in range(3)
        ]

    def all_sum(iteration, value):
        for number in range(ROUNDS):
            at = iteration * ROUNDS + number
            count = len(peers[number])
            sum_out[at] = value
            def give(devices):
                for step, device in enumerate(devices):
                    remote(sum_out.at[at], sum_in.at[at, step], sum_send.at[at], sum_recv.at[at], device)

            if number == 0:
                give(peers[0])
            else:

                @pl.when(g % 2 == 1)
                def _():
                    for step, (layer, cell) in enumerate(peers[1]):
                        for target in (layer - 1, layer):
                            remote(sum_out.at[at], sum_in.at[at, step], sum_send.at[at], sum_recv.at[at], (target, cell))

            landed = sum_in.at[at, pl.ds(0, count)]
            pltpu.make_async_copy(landed, landed, sum_recv.at[at]).wait()
            terms = [value] + [sum_in[at, step] for step in range(count)]
            while len(terms) > 1:
                pairs = [a + b for a, b in zip(terms[::2], terms[1::2])]
                terms = pairs + terms[2 * len(pairs) :]
            value = terms[0]
        return value

    pass_token(0)
    factors = momentum_factors(ITERS)
    current = [alive * impulses_ref[r] for r in range(3)]
    earlier = [alive * previous_ref[r] for r in range(3)]
    guess = [alive * (current[r] + factors[0] * (current[r] - earlier[r])) for r in range(3)]
    for iteration in range(ITERS):
        phase = 3 * iteration
        velocity = free + weights * collect(phase, guess, set_halo if iteration == 0 else None)
        if iteration == 0:
            pl.semaphore_wait(token_sems.at[0], len(tokens[0]))
            pass_token(1)
        rows = rows_of(phase + 1, velocity)
        rows[0] = rows[0] + offset
        gradient = [alive * (rows[r] + softness * guess[r]) for r in range(3)]
        squares = gradient[0] * gradient[0] + gradient[1] * gradient[1] + gradient[2] * gradient[2]
        norm = lanes(squares)
        soft = lanes(softness * squares)
        sums = collect(phase + 2, gradient)
        if iteration == 0:
            pl.semaphore_wait(token_sems.at[1], len(tokens[1]))
        curve = jnp.sum(lanes(weights * sums * sums), axis=0, keepdims=True) + soft
        value = all_sum(iteration, jnp.concatenate([norm, curve], axis=0))
        total = jnp.sum(value, axis=1, keepdims=True)
        step_size = total[0:1] / (total[1:2] + EPSILON)
        moved = [guess[r] - step_size * gradient[r] for r in range(3)]
        updated = [alive * v for v in cone_project(moved[0], moved[1], moved[2], friction)]
        if iteration + 1 < ITERS:
            guess = [
                alive * (updated[r] + factors[iteration + 1] * (updated[r] - current[r]))
                for r in range(3)
            ]
        current = updated
    for r in range(3):
        impulses_out[r] = current[r]
    final = free + weights * collect(PHASES - 1, current)
    for j in range(6):
        velocity_out[j] = final[j : j + 1, :]

    @pl.when(has_above)
    def _():
        pltpu.make_async_copy(side_out, side_out, side_sems.at[0]).wait()

    for phase in range(PHASES):
        await_segments(phase, phase_send, downward if phase in SPREADS else upward)
    for at in range(ITERS * ROUNDS):
        gone = sum_in.at[at, pl.ds(0, len(peers[0]) if at % ROUNDS == 0 else 2 * len(peers[1]))]

        @pl.when(jnp.logical_or(at % ROUNDS == 0, g % 2 == 1))
        def _():
            pltpu.make_async_copy(gone, gone, sum_send.at[at]).wait()


def solution(mesh):
    layers, cells = mesh.shape["gz"], mesh.shape["xy"]
    depth = 16

    def on_device(
        velocity_free,
        inverse_mass,
        jacobian,
        impulses,
        previous_impulses,
        compliance,
        offset,
        friction,
        body_near,
        body_far,
        block_counts,
        layer_send,
        side_send,
    ):
        own = velocity_free.shape[3]
        contacts = jacobian.shape[3]
        vmem = pl.BlockSpec(memory_space=pltpu.VMEM)
        sums = ITERS * ROUNDS
        partners = max(layers * (cells // depth), depth) - 1
        operands = (
            velocity_free.reshape(6, 1, own),
            inverse_mass[0, 0],
            jacobian.reshape(36 * contacts // 128, 128),
            impulses.reshape(3, 1, contacts),
            previous_impulses.reshape(3, 1, contacts),
            compliance[0],
            offset[0],
            friction[0],
            body_near[0],
            body_far[0],
            block_counts[0],
            layer_send[0],
            side_send[0, 0],
        )
        outs = pl.pallas_call(
            functools.partial(kernel, layers, cells, depth),
            out_shape=(
                jax.ShapeDtypeStruct((3, 1, contacts), F32),
                jax.ShapeDtypeStruct((6, 1, own), F32),
            ),
            in_specs=[pl.BlockSpec(memory_space=pl.ANY)] * 13,
            out_specs=(vmem, vmem),
            scratch_shapes=[
                pltpu.VMEM((WIDE, contacts), BF16),
                pltpu.VMEM((2, 16, contacts), BF16),
                pltpu.VMEM((WIDE, contacts), BF16),
                pltpu.VMEM((5, 16, contacts), BF16),
                pltpu.VMEM((WIDE, 5 * WIDE), BF16),
                pltpu.VMEM((2, 16, 5 * WIDE), BF16),
                pltpu.VMEM((3, 8, contacts), F32),
                pltpu.VMEM((3, 8, contacts), F32),
                pltpu.VMEM((8, 2 * WIDE), F32),
                pltpu.VMEM((8, 2 * WIDE), F32),
                pltpu.VMEM((PHASES, 8, 5 * WIDE), F32),
                pltpu.VMEM((PHASES, 8, 5 * WIDE), F32),
                pltpu.VMEM((sums, 2, 128), F32),
                pltpu.VMEM((sums, partners, 2, 128), F32),
                pltpu.SemaphoreType.DMA((2,)),
                pltpu.SemaphoreType.DMA((PHASES,)),
                pltpu.SemaphoreType.DMA((PHASES,)),
                pltpu.SemaphoreType.DMA((sums,)),
                pltpu.SemaphoreType.DMA((sums,)),
                pltpu.SemaphoreType.REGULAR((2,)),
                *[pltpu.VMEM(v.shape, v.dtype) for v in operands],
                pltpu.SemaphoreType.DMA((len(operands),)),
            ],
            compiler_params=pltpu.CompilerParams(
                collective_id=0, has_side_effects=True, vmem_limit_bytes=56 << 20
            ),
        )(*operands)
        return outs[0].reshape(1, 1, 3, contacts), outs[1].reshape(1, 1, 6, own)

    field = P("gz", "xy", None, None)
    line = P("gz", "xy", None)
    return jax.shard_map(
        on_device,
        mesh=mesh,
        in_specs=(field,) * 5 + (line,) * 7 + (field,),
        out_specs=(field, field),
        check_vma=False,
    )
```

```python
import functools
import math

import jax
import jax.numpy as jnp
from jax import lax
from jax.experimental import pallas as pl
from jax.experimental.pallas import tpu as pltpu
from jax.sharding import PartitionSpec as P

ITERS = 2
EPSILON = 1e-06
THETA_START = 0.3

MESH = pl.DeviceIdType.MESH
F32 = jnp.float32
BF16 = jnp.bfloat16
WIDE = 256
PHASES = 3 * ITERS + 1
SPREADS = tuple(3 * iteration + 1 for iteration in range(ITERS))
ROUNDS = 2


def theta_after(theta_value):
    return 0.5 * (
        -theta_value * theta_value + theta_value * math.sqrt(theta_value * theta_value + 4.0)
    )


def momentum_factors(iteration_count):
    thetas = [THETA_START]
    for iteration in range(iteration_count):
        thetas.append(theta_after(thetas[-1]))
    return [
        thetas[position]
        * (1.0 - thetas[position])
        / (thetas[position] * thetas[position] + thetas[position + 1])
        for position in range(iteration_count)
    ]


def halves(rows):
    high = rows.astype(BF16).astype(F32)
    return jnp.concatenate([high, rows - high], axis=0).astype(BF16)


def set_hot(index, hot_ref, mask_ref):
    lane = jnp.where(index < 0, -1, index & (WIDE - 1))
    tile = index >> 8
    width = index.shape[1]
    for start in range(0, width, WIDE):
        part = lane[:, start : start + WIDE]
        row = lax.broadcasted_iota(jnp.int32, (WIDE, WIDE), 0)
        hot_ref[:, start : start + WIDE] = (row == part).astype(F32).astype(BF16)
    for number in range(mask_ref.shape[0]):
        mask = (tile == number).astype(F32)
        mask_ref[number] = jnp.broadcast_to(mask, (16, width)).astype(BF16)


def scatter(both, numbers, hot_ref, mask_ref):
    left = jnp.concatenate([both * mask_ref[number] for number in numbers], axis=0)
    sums = lax.dot_general(
        left, hot_ref[...], (((1,), (1,)), ((), ())), preferred_element_type=F32
    )
    return [
        sums[16 * i : 16 * i + 8] + sums[16 * i + 8 : 16 * i + 16]
        for i in range(len(numbers))
    ]


def gather(tiles, numbers, hot_ref, mask_ref):
    left = jnp.concatenate([halves(tile) for tile in tiles], axis=0)
    found = jnp.dot(left, hot_ref[...], preferred_element_type=F32)
    total = None
    for position, number in enumerate(numbers):
        part = found[16 * position : 16 * position + 8] + found[16 * position + 8 : 16 * position + 16]
        part = part * mask_ref[number][:8].astype(F32)
        total = part if total is None else total + part
    return total


def lanes(row):
    total = row[:, :128]
    for start in range(128, row.shape[1], 128):
        total = total + row[:, start : start + 128]
    return total


def cone_project(normal, first, second, friction):
    slide = jnp.sqrt(first * first + second * second)
    inside = slide <= friction * normal
    polar = friction * slide <= -normal
    outside = jnp.logical_not(jnp.logical_or(inside, polar))
    onto = (friction * slide + normal) / (friction * friction + 1.0)
    scale = friction * onto / jnp.where(outside, slide, 1.0)
    scale = jnp.where(inside, 1.0, jnp.where(polar, 0.0, scale))
    new_normal = jnp.where(inside, normal, jnp.where(polar, 0.0, onto))
    return [new_normal, scale * first, scale * second]


def kernel(
    layers,
    cells,
    depth,
    free_hbm,
    mass_hbm,
    jacobian_hbm,
    impulses_hbm,
    previous_hbm,
    compliance_hbm,
    offset_hbm,
    friction_hbm,
    near_hbm,
    far_hbm,
    counts_hbm,
    layer_hbm,
    side_hbm,
    impulses_out,
    velocity_out,
    near_hot,
    near_mask,
    far_hot,
    far_mask,
    halo_hot,
    halo_mask,
    near_jac,
    far_jac,
    side_out,
    side_in,
    sent,
    received,
    sum_out,
    sum_in,
    side_sems,
    phase_send,
    phase_recv,
    sum_send,
    sum_recv,
    token_sems,
    free_ref,
    mass_ref,
    jacobian_ref,
    impulses_ref,
    previous_ref,
    compliance_ref,
    offset_ref,
    friction_ref,
    near_ref,
    far_ref,
    counts_ref,
    layer_ref,
    side_ref,
    load_sems,
):
    g = lax.axis_index("gz")
    x = lax.axis_index("xy")
    has_below, has_above = g > 0, g < layers - 1
    has_lower, has_higher = x > 0, x < cells - 1
    beside = has_lower.astype(jnp.int32) + has_higher.astype(jnp.int32)
    upward = beside + jnp.where(has_above, beside + 1, 0)
    downward = beside + jnp.where(has_below, beside + 1, 0)
    below, above = (g + layers - 1) % layers, (g + 1) % layers
    lower, higher = (x + cells - 1) % cells, (x + 1) % cells
    line = x // depth * depth
    odd = g % 2 == 1
    plane = [
        ((g // 2 * 2 + 1 + 2 * step) % layers, (x + depth * stride) % cells)
        for step in (2, 1, 3, 0)
        for stride in (2, 1, 3, 0)
    ]
    column = [
        (g, line + (x - line + step) % depth)
        for step in sorted(range(1, depth), key=lambda step: -min(step, depth - step))
    ]
    around = [
        (g, lower),
        (g, higher),
        (below, x),
        (above, x),
        (below, lower),
        (below, higher),
        (above, lower),
        (above, higher),
    ]

    loads = [
        pltpu.make_async_copy(source, target, load_sems.at[number])
        for number, (source, target) in enumerate(
            (
                (far_hbm, far_ref),
                (near_hbm, near_ref),
                (side_hbm, side_ref),
                (jacobian_hbm, jacobian_ref),
                (impulses_hbm, impulses_ref),
                (previous_hbm, previous_ref),
                (counts_hbm, counts_ref),
                (layer_hbm, layer_ref),
                (free_hbm, free_ref),
                (mass_hbm, mass_ref),
                (compliance_hbm, compliance_ref),
                (offset_hbm, offset_ref),
                (friction_hbm, friction_ref),
            )
        )
    ]
    for load in loads:
        load.start()

    received[...] = jnp.zeros_like(received)
    side_in[...] = jnp.full_like(side_in, -1.0)

    barrier = pltpu.get_barrier_semaphore()
    def along(step):
        return (g, line + (x - line + step) % depth)

    def across(step):
        return (g, (x + depth * step) % cells)

    def through(step):
        return ((g + step) % layers, x)

    both_ways = lambda place, *steps: [place(step) for near in steps for step in (near, -near)]
    greeted = around + both_ways(through, 2) + both_ways(across, 1) + both_ways(along, 1, 2)
    tokens = [
        both_ways(through, 2) + both_ways(across, 1) + both_ways(along, 2),
        both_ways(across, 1) + [across(2)] + both_ways(along, 4),
    ]
    for device in greeted:
        pl.semaphore_signal(barrier, inc=1, device_id=device, device_id_type=MESH)

    def remote(src, dst, send_sem, recv_sem, device):
        copy = pltpu.make_async_remote_copy(
            src_ref=src,
            dst_ref=dst,
            send_sem=send_sem,
            recv_sem=recv_sem,
            device_id=device,
            device_id_type=MESH,
        )
        copy.start()

    for load in loads:
        load.wait()
    slabs = near_jac.shape[2] // 128
    near_jac[...] = jnp.zeros_like(near_jac)
    far_jac[...] = jnp.zeros_like(far_jac)
    for r in range(3):
        for t in range(slabs):
            columns = slice(128 * t, 128 * t + 128)
            near_jac[r, 0:6, columns] = jacobian_ref[pl.ds(12 * r * slabs + t, 6, slabs), :]
            far_jac[r, 0:6, columns] = jacobian_ref[pl.ds((12 * r + 6) * slabs + t, 6, slabs), :]
    side_rows = side_ref.shape[1]
    side_list = side_ref[...].astype(F32)
    pad = jnp.full((1, WIDE - side_rows), -1.0, F32)
    side_row = jnp.concatenate([side_list[0:1], pad, side_list[1:2], pad], axis=1)
    side_out[...] = jnp.broadcast_to(side_row, side_out.shape)

    own = free_ref.shape[2]
    layer_rows = layer_ref.shape[1]
    section = own + layer_rows
    far = far_ref[...]
    far = jnp.where(
        far < section, far, jnp.where(far < section + side_rows, far + (3 * WIDE - section), far + (4 * WIDE - section - side_rows))
    )
    set_hot(far, far_hot, far_mask)

    pl.semaphore_wait(barrier, len(greeted))
    @pl.when(has_above)
    def _():
        remote(side_out, side_in, side_sems.at[0], side_sems.at[1], (above, x))

    slot = lax.broadcasted_iota(jnp.int32, (1, 128), 1)
    counts = counts_ref[...]
    alive = jnp.concatenate(
        [(slot < counts[:, b : b + 1]).astype(F32) for b in range(counts.shape[1])], axis=1
    )
    softness = compliance_ref[...]
    friction = friction_ref[...]
    offset = offset_ref[...]
    sphere_row = lax.broadcasted_iota(jnp.int32, (8, own), 0)
    weights = jnp.where(
        sphere_row < 3, mass_ref[0:1, :], jnp.where(sphere_row < 6, mass_ref[1:2, :], 0.0)
    )
    free = jnp.concatenate([free_ref[j] for j in range(6)] + [jnp.zeros((2, own), F32)], axis=0)

    def set_near():
        set_hot(near_ref[...], near_hot, near_mask)

    def set_halo():
        @pl.when(has_below)
        def _():
            pltpu.make_async_copy(side_in, side_in, side_sems.at[1]).wait()

        layer = layer_ref[...]
        other = side_in[0:1, :].astype(jnp.int32)
        relative = other - own
        row = lax.broadcasted_iota(jnp.int32, (layer_rows, 2 * WIDE), 0)
        hot = (row == relative).astype(F32).astype(BF16)
        parts = jnp.concatenate(
            [jnp.broadcast_to(layer >> 8, (8, layer_rows)), jnp.broadcast_to(layer & 255, (8, layer_rows))], axis=0
        )
        found = jnp.dot(parts.astype(F32).astype(BF16), hot, preferred_element_type=F32)
        composed = (found[0:1] * 256.0 + found[8:9]).astype(jnp.int32)
        composed = jnp.where(relative >= 0, composed, -1)
        mine = side_row.astype(jnp.int32)
        mine = jnp.where(mine < own, mine, -1)
        bottom, first, last = g == 0, x == 0, x == cells - 1
        none = jnp.full((1, WIDE), -1, jnp.int32)
        to_layer = jnp.concatenate([layer, jnp.full((1, WIDE - layer_rows), -1, jnp.int32)], axis=1)
        index = jnp.concatenate(
            [
                jnp.where(bottom, none, to_layer),
                jnp.where(first, none, mine[:, :WIDE]),
                jnp.where(last, none, mine[:, WIDE:]),
                jnp.where(jnp.logical_or(bottom, first), none, composed[:, :WIDE]),
                jnp.where(jnp.logical_or(bottom, last), none, composed[:, WIDE:]),
            ],
            axis=1,
        )
        set_hot(index, halo_hot, halo_mask)

    def part(ref, phase, number):
        return ref.at[phase, :, pl.ds(number * WIDE, WIDE)]

    def pass_token(number):
        for device in tokens[number]:
            pl.semaphore_signal(token_sems.at[number], inc=1, device_id=device, device_id_type=MESH)

    def send(phase, number, segment, device, valid):
        @pl.when(valid)
        def _():
            remote(
                part(sent, phase, number),
                part(received, phase, segment),
                phase_send.at[phase],
                phase_recv.at[phase],
                device,
            )

    def await_segments(phase, sem, count):
        for number in (1, 2, 3, 5):

            @pl.when(count == number)
            def _():
                moved = received.at[phase, :, pl.ds(0, number * WIDE)]
                pltpu.make_async_copy(moved, moved, sem.at[phase]).wait()

    def collect(phase, impulse, ready=None, between=None):
        far_terms = far_jac[0] * impulse[0] + far_jac[1] * impulse[1] + far_jac[2] * impulse[2]
        far_terms = halves(far_terms)
        leaving = scatter(far_terms, (2, 3, 4), far_hot, far_mask)
        for number in range(3):
            sent[phase, :, number * WIDE : (number + 1) * WIDE] = leaving[number]
        send(phase, 1, 4, (above, lower), jnp.logical_and(has_above, has_lower))
        send(phase, 2, 3, (above, higher), jnp.logical_and(has_above, has_higher))
        send(phase, 1, 2, (g, lower), has_lower)
        send(phase, 2, 1, (g, higher), has_higher)
        send(phase, 0, 0, (above, x), has_above)
        if ready is not None:
            ready()
        near_terms = near_jac[0] * impulse[0] + near_jac[1] * impulse[1] + near_jac[2] * impulse[2]
        near_tiles = scatter(halves(near_terms), (0, 1), near_hot, near_mask)
        far_tiles = scatter(far_terms, (0, 1), far_hot, far_mask)
        if between is not None:
            between()
        await_segments(phase, phase_recv, downward)
        halo_tiles = scatter(halves(received[phase]), (0, 1), halo_hot, halo_mask)
        return jnp.concatenate(
            [far_tiles[i] + near_tiles[i] + halo_tiles[i] for i in range(2)], axis=1
        )

    def rows_of(phase, velocity):
        own_tiles = [velocity[:, :WIDE], velocity[:, WIDE:]]
        sent[phase] = gather(own_tiles, range(2), halo_hot, halo_mask)
        send(phase, 3, 3, (below, lower), jnp.logical_and(has_below, has_lower))
        send(phase, 4, 4, (below, higher), jnp.logical_and(has_below, has_higher))
        send(phase, 1, 1, (g, lower), has_lower)
        send(phase, 2, 2, (g, higher), has_higher)
        send(phase, 0, 0, (below, x), has_below)
        near_rows = gather(own_tiles, range(2), near_hot, near_mask)
        far_rows = gather(own_tiles, range(2), far_hot, far_mask)
        partial = [near_jac[r] * near_rows for r in range(3)]
        await_segments(phase, phase_recv, upward)
        segments = [received[phase, :, i * WIDE : (i + 1) * WIDE] for i in range(5)]
        far_rows = far_rows + gather(
            [segments[0], segments[2] + segments[4], segments[1] + segments[3]], (2, 3, 4), far_hot, far_mask
        )
        return [
            jnp.sum(partial[r] + far_jac[r] * far_rows, axis=0, keepdims=True) for r in range(3)
        ]

    def tree(terms):
        while len(terms) > 1:
            pairs = [a + b for a, b in zip(terms[::2], terms[1::2])]
            terms = pairs + terms[2 * len(pairs) :]
        return terms[0]

    def rows_moved(at, sem, count):
        moved = sum_in.at[at, pl.ds(0, count)]
        pltpu.make_async_copy(moved, moved, sem.at[at]).wait()

    def give(at, slot, device):
        remote(sum_out.at[at], sum_in.at[at, slot], sum_send.at[at], sum_recv.at[at], device)

    def all_sum(iteration, value):
        at = iteration * ROUNDS
        sum_out[at] = value
        within = len(plane)

        @pl.when(odd)
        def _():
            for slot, device in enumerate(plane[:-1]):
                give(at, within + slot, device)
            rows_moved(at, sum_recv, 2 * within - 1)
            sum_out[at + 1] = tree([value] + [sum_in[at, slot] for slot in range(2 * within - 1)])
            for slot, (layer, cell) in enumerate(column):
                give(at + 1, slot, (layer - 1, cell))
                give(at + 1, slot, (layer, cell))
            give(at + 1, len(column), (g - 1, x))
            rows_moved(at + 1, sum_recv, len(column))

        @pl.when(jnp.logical_not(odd))
        def _():
            for slot, device in enumerate(plane):
                give(at, slot, device)
            rows_moved(at + 1, sum_recv, len(column) + 1)
            sum_out[at + 1] = sum_in[at + 1, len(column)]

        return tree([sum_out[at + 1]] + [sum_in[at + 1, slot] for slot in range(len(column))])

    pass_token(0)
    factors = momentum_factors(ITERS)
    current = [alive * impulses_ref[r] for r in range(3)]
    earlier = [alive * previous_ref[r] for r in range(3)]
    guess = [alive * (current[r] + factors[0] * (current[r] - earlier[r])) for r in range(3)]
    for iteration in range(ITERS):
        phase = 3 * iteration
        velocity = free + weights * collect(phase, guess, *((set_near, set_halo) if iteration == 0 else ()))
        if iteration == 0:
            pl.semaphore_wait(token_sems.at[0], len(tokens[0]))
            pass_token(1)
        rows = rows_of(phase + 1, velocity)
        rows[0] = rows[0] + offset
        gradient = [alive * (rows[r] + softness * guess[r]) for r in range(3)]
        squares = gradient[0] * gradient[0] + gradient[1] * gradient[1] + gradient[2] * gradient[2]
        norm = lanes(squares)
        soft = lanes(softness * squares)
        sums = collect(phase + 2, gradient)
        if iteration == 0:
            pl.semaphore_wait(token_sems.at[1], len(tokens[1]))
        curve = jnp.sum(lanes(weights * sums * sums), axis=0, keepdims=True) + soft
        value = all_sum(iteration, jnp.concatenate([norm, curve], axis=0))
        total = jnp.sum(value, axis=1, keepdims=True)
        step_size = total[0:1] / (total[1:2] + EPSILON)
        moved = [guess[r] - step_size * gradient[r] for r in range(3)]
        updated = [alive * v for v in cone_project(moved[0], moved[1], moved[2], friction)]
        if iteration + 1 < ITERS:
            guess = [
                alive * (updated[r] + factors[iteration + 1] * (updated[r] - current[r]))
                for r in range(3)
            ]
        current = updated
    for r in range(3):
        impulses_out[r] = current[r]
    final = free + weights * collect(PHASES - 1, current)
    for j in range(6):
        velocity_out[j] = final[j : j + 1, :]

    @pl.when(has_above)
    def _():
        pltpu.make_async_copy(side_out, side_out, side_sems.at[0]).wait()

    for phase in range(PHASES):
        await_segments(phase, phase_send, downward if phase in SPREADS else upward)
    for iteration in range(ITERS):
        at = iteration * ROUNDS

        @pl.when(odd)
        def _():
            rows_moved(at, sum_send, len(plane) - 1)
            rows_moved(at + 1, sum_send, 2 * len(column) + 1)

        @pl.when(jnp.logical_not(odd))
        def _():
            rows_moved(at, sum_send, len(plane))


def solution(mesh):
    layers, cells = mesh.shape["gz"], mesh.shape["xy"]
    depth = 16

    def on_device(
        velocity_free,
        inverse_mass,
        jacobian,
        impulses,
        previous_impulses,
        compliance,
        offset,
        friction,
        body_near,
        body_far,
        block_counts,
        layer_send,
        side_send,
    ):
        own = velocity_free.shape[3]
        contacts = jacobian.shape[3]
        vmem = pl.BlockSpec(memory_space=pltpu.VMEM)
        sums = ITERS * ROUNDS
        partners = max(layers * (cells // depth), depth) - 1
        operands = (
            velocity_free.reshape(6, 1, own),
            inverse_mass[0, 0],
            jacobian.reshape(36 * contacts // 128, 128),
            impulses.reshape(3, 1, contacts),
            previous_impulses.reshape(3, 1, contacts),
            compliance[0],
            offset[0],
            friction[0],
            body_near[0],
            body_far[0],
            block_counts[0],
            layer_send[0],
            side_send[0, 0],
        )
        outs = pl.pallas_call(
            functools.partial(kernel, layers, cells, depth),
            out_shape=(
                jax.ShapeDtypeStruct((3, 1, contacts), F32),
                jax.ShapeDtypeStruct((6, 1, own), F32),
            ),
            in_specs=[pl.BlockSpec(memory_space=pl.ANY)] * 13,
            out_specs=(vmem, vmem),
            scratch_shapes=[
                pltpu.VMEM((WIDE, contacts), BF16),
                pltpu.VMEM((2, 16, contacts), BF16),
                pltpu.VMEM((WIDE, contacts), BF16),
                pltpu.VMEM((5, 16, contacts), BF16),
                pltpu.VMEM((WIDE, 5 * WIDE), BF16),
                pltpu.VMEM((2, 16, 5 * WIDE), BF16),
                pltpu.VMEM((3, 8, contacts), F32),
                pltpu.VMEM((3, 8, contacts), F32),
                pltpu.VMEM((8, 2 * WIDE), F32),
                pltpu.VMEM((8, 2 * WIDE), F32),
                pltpu.VMEM((PHASES, 8, 5 * WIDE), F32),
                pltpu.VMEM((PHASES, 8, 5 * WIDE), F32),
                pltpu.VMEM((sums, 2, 128), F32),
                pltpu.VMEM((sums, partners, 2, 128), F32),
                pltpu.SemaphoreType.DMA((2,)),
                pltpu.SemaphoreType.DMA((PHASES,)),
                pltpu.SemaphoreType.DMA((PHASES,)),
                pltpu.SemaphoreType.DMA((sums,)),
                pltpu.SemaphoreType.DMA((sums,)),
                pltpu.SemaphoreType.REGULAR((2,)),
                *[pltpu.VMEM(v.shape, v.dtype) for v in operands],
                pltpu.SemaphoreType.DMA((len(operands),)),
            ],
            compiler_params=pltpu.CompilerParams(
                collective_id=0, has_side_effects=True, vmem_limit_bytes=56 << 20
            ),
        )(*operands)
        return outs[0].reshape(1, 1, 3, contacts), outs[1].reshape(1, 1, 6, own)

    field = P("gz", "xy", None, None)
    line = P("gz", "xy", None)
    return jax.shard_map(
        on_device,
        mesh=mesh,
        in_specs=(field,) * 5 + (line,) * 7 + (field,),
        out_specs=(field, field),
        check_vma=False,
    )
```

```python
import functools
import math

import jax
import jax.numpy as jnp
from jax import lax
from jax.experimental import pallas as pl
from jax.experimental.pallas import tpu as pltpu
from jax.sharding import PartitionSpec as P

ITERS = 2
EPSILON = 1e-06
THETA_START = 0.3

MESH = pl.DeviceIdType.MESH
F32 = jnp.float32
BF16 = jnp.bfloat16
WIDE = 256
PHASES = 3 * ITERS + 1
SPREADS = tuple(3 * iteration + 1 for iteration in range(ITERS))
ROUNDS = 2


def theta_after(theta_value):
    return 0.5 * (
        -theta_value * theta_value + theta_value * math.sqrt(theta_value * theta_value + 4.0)
    )


def momentum_factors(iteration_count):
    thetas = [THETA_START]
    for iteration in range(iteration_count):
        thetas.append(theta_after(thetas[-1]))
    return [
        thetas[position]
        * (1.0 - thetas[position])
        / (thetas[position] * thetas[position] + thetas[position + 1])
        for position in range(iteration_count)
    ]


def halves(rows):
    high = rows.astype(BF16).astype(F32)
    return jnp.concatenate([high, rows - high], axis=0).astype(BF16)


def set_hot(index, hot_ref, mask_ref):
    lane = jnp.where(index < 0, -1, index & (WIDE - 1))
    tile = index >> 8
    width = index.shape[1]
    for start in range(0, width, WIDE):
        part = lane[:, start : start + WIDE]
        row = lax.broadcasted_iota(jnp.int32, (WIDE, WIDE), 0)
        hot_ref[:, start : start + WIDE] = (row == part).astype(F32).astype(BF16)
    for number in range(mask_ref.shape[0]):
        mask = (tile == number).astype(F32)
        mask_ref[number] = jnp.broadcast_to(mask, (16, width)).astype(BF16)


def scatter(both, numbers, hot_ref, mask_ref):
    left = jnp.concatenate([both * mask_ref[number] for number in numbers], axis=0)
    sums = lax.dot_general(
        left, hot_ref[...], (((1,), (1,)), ((), ())), preferred_element_type=F32
    )
    return [
        sums[16 * i : 16 * i + 8] + sums[16 * i + 8 : 16 * i + 16]
        for i in range(len(numbers))
    ]


def gather(tiles, numbers, hot_ref, mask_ref):
    left = jnp.concatenate([halves(tile) for tile in tiles], axis=0)
    found = jnp.dot(left, hot_ref[...], preferred_element_type=F32)
    total = None
    for position, number in enumerate(numbers):
        part = found[16 * position : 16 * position + 8] + found[16 * position + 8 : 16 * position + 16]
        part = part * mask_ref[number][:8].astype(F32)
        total = part if total is None else total + part
    return total


def lanes(row):
    total = row[:, :128]
    for start in range(128, row.shape[1], 128):
        total = total + row[:, start : start + 128]
    return total


def cone_project(normal, first, second, friction):
    slide = jnp.sqrt(first * first + second * second)
    inside = slide <= friction * normal
    polar = friction * slide <= -normal
    outside = jnp.logical_not(jnp.logical_or(inside, polar))
    onto = (friction * slide + normal) / (friction * friction + 1.0)
    scale = friction * onto / jnp.where(outside, slide, 1.0)
    scale = jnp.where(inside, 1.0, jnp.where(polar, 0.0, scale))
    new_normal = jnp.where(inside, normal, jnp.where(polar, 0.0, onto))
    return [new_normal, scale * first, scale * second]


def kernel(
    layers,
    cells,
    depth,
    free_hbm,
    mass_hbm,
    jacobian_hbm,
    impulses_hbm,
    previous_hbm,
    compliance_hbm,
    offset_hbm,
    friction_hbm,
    near_hbm,
    far_hbm,
    counts_hbm,
    layer_hbm,
    side_hbm,
    impulses_out,
    velocity_out,
    near_hot,
    near_mask,
    far_hot,
    far_mask,
    halo_hot,
    halo_mask,
    near_jac,
    far_jac,
    side_out,
    side_in,
    sent,
    received,
    sum_out,
    sum_in,
    side_sems,
    phase_send,
    phase_recv,
    sum_send,
    sum_recv,
    token_sems,
    free_ref,
    mass_ref,
    jacobian_ref,
    impulses_ref,
    previous_ref,
    compliance_ref,
    offset_ref,
    friction_ref,
    near_ref,
    far_ref,
    counts_ref,
    layer_ref,
    side_ref,
    load_sems,
):
    g = lax.axis_index("gz")
    x = lax.axis_index("xy")
    has_below, has_above = g > 0, g < layers - 1
    has_lower, has_higher = x > 0, x < cells - 1
    beside = has_lower.astype(jnp.int32) + has_higher.astype(jnp.int32)
    upward = beside + jnp.where(has_above, beside + 1, 0)
    downward = beside + jnp.where(has_below, beside + 1, 0)
    below, above = (g + layers - 1) % layers, (g + 1) % layers
    lower, higher = (x + cells - 1) % cells, (x + 1) % cells
    line = x // depth * depth
    odd = g % 2 == 1
    plane = [
        ((g // 2 * 2 + 1 + 2 * step) % layers, (x + depth * stride) % cells)
        for step in (2, 1, 3, 0)
        for stride in (2, 1, 3, 0)
    ]
    column = [
        (g, line + (x - line + step) % depth)
        for step in sorted(range(1, depth), key=lambda step: -min(step, depth - step))
    ]
    around = [
        (g, lower),
        (g, higher),
        (below, x),
        (above, x),
        (below, lower),
        (below, higher),
        (above, lower),
        (above, higher),
    ]

    loads = [
        pltpu.make_async_copy(source, target, load_sems.at[number])
        for number, (source, target) in enumerate(
            (
                (far_hbm, far_ref),
                (near_hbm, near_ref),
                (side_hbm, side_ref),
                (jacobian_hbm, jacobian_ref.at[pl.ds(0, jacobian_hbm.shape[0])]),
                (impulses_hbm, impulses_ref),
                (previous_hbm, previous_ref),
                (counts_hbm, counts_ref),
                (layer_hbm, layer_ref),
                (free_hbm, free_ref),
                (mass_hbm, mass_ref),
                (compliance_hbm, compliance_ref),
                (offset_hbm, offset_ref),
                (friction_hbm, friction_ref),
            )
        )
    ]
    for load in loads:
        load.start()

    received[...] = jnp.zeros_like(received)
    side_in[...] = jnp.full_like(side_in, -1.0)

    barrier = pltpu.get_barrier_semaphore()
    def along(step):
        return (g, line + (x - line + step) % depth)

    def across(step):
        return (g, (x + depth * step) % cells)

    def through(step):
        return ((g + step) % layers, x)

    both_ways = lambda place, *steps: [place(step) for near in steps for step in (near, -near)]
    greeted = around + both_ways(through, 2) + both_ways(across, 1) + both_ways(along, 1, 2)
    tokens = [
        both_ways(through, 2) + both_ways(across, 1) + both_ways(along, 2),
        both_ways(across, 1) + [across(2)] + both_ways(along, 4),
    ]
    for device in greeted:
        pl.semaphore_signal(barrier, inc=1, device_id=device, device_id_type=MESH)

    def remote(src, dst, send_sem, recv_sem, device):
        copy = pltpu.make_async_remote_copy(
            src_ref=src,
            dst_ref=dst,
            send_sem=send_sem,
            recv_sem=recv_sem,
            device_id=device,
            device_id_type=MESH,
        )
        copy.start()

    for load in loads:
        load.wait()
    slabs = near_jac.shape[2] // 128
    near_jac[...] = jnp.zeros_like(near_jac)
    far_jac[...] = jnp.zeros_like(far_jac)
    for r in range(3):
        for t in range(slabs):
            columns = slice(128 * t, 128 * t + 128)
            near_jac[r, 0:6, columns] = jacobian_ref[pl.ds(12 * r * slabs + t, 6, slabs), :]
            far_jac[r, 0:6, columns] = jacobian_ref[pl.ds((12 * r + 6) * slabs + t, 6, slabs), :]
    side_rows = side_ref.shape[1]
    side_list = side_ref[...].astype(F32)
    pad = jnp.full((1, WIDE - side_rows), -1.0, F32)
    side_row = jnp.concatenate([side_list[0:1], pad, side_list[1:2], pad], axis=1)
    side_out[...] = jnp.broadcast_to(side_row, side_out.shape)

    own = free_ref.shape[2]
    layer_rows = layer_ref.shape[1]
    section = own + layer_rows
    far = far_ref[...]
    far = jnp.where(
        far < section, far, jnp.where(far < section + side_rows, far + (3 * WIDE - section), far + (4 * WIDE - section - side_rows))
    )
    set_hot(far, far_hot, far_mask)

    pl.semaphore_wait(barrier, len(greeted))
    @pl.when(has_above)
    def _():
        remote(side_out, side_in, side_sems.at[0], side_sems.at[1], (above, x))

    slot = lax.broadcasted_iota(jnp.int32, (1, 128), 1)
    counts = counts_ref[...]
    alive = jnp.concatenate(
        [(slot < counts[:, b : b + 1]).astype(F32) for b in range(counts.shape[1])], axis=1
    )
    softness = compliance_ref[...]
    friction = friction_ref[...]
    offset = offset_ref[...]
    sphere_row = lax.broadcasted_iota(jnp.int32, (8, own), 0)
    weights = jnp.where(
        sphere_row < 3, mass_ref[0:1, :], jnp.where(sphere_row < 6, mass_ref[1:2, :], 0.0)
    )
    free = jnp.concatenate([free_ref[j] for j in range(6)] + [jnp.zeros((2, own), F32)], axis=0)

    def set_near():
        set_hot(near_ref[...], near_hot, near_mask)

    def set_halo():
        @pl.when(has_below)
        def _():
            pltpu.make_async_copy(side_in, side_in, side_sems.at[1]).wait()

        layer = layer_ref[...]
        other = side_in[0:1, :].astype(jnp.int32)
        relative = other - own
        row = lax.broadcasted_iota(jnp.int32, (layer_rows, 2 * WIDE), 0)
        hot = (row == relative).astype(F32).astype(BF16)
        parts = jnp.concatenate(
            [jnp.broadcast_to(layer >> 8, (8, layer_rows)), jnp.broadcast_to(layer & 255, (8, layer_rows))], axis=0
        )
        found = jnp.dot(parts.astype(F32).astype(BF16), hot, preferred_element_type=F32)
        composed = (found[0:1] * 256.0 + found[8:9]).astype(jnp.int32)
        composed = jnp.where(relative >= 0, composed, -1)
        mine = side_row.astype(jnp.int32)
        mine = jnp.where(mine < own, mine, -1)
        bottom, first, last = g == 0, x == 0, x == cells - 1
        none = jnp.full((1, WIDE), -1, jnp.int32)
        to_layer = jnp.concatenate([layer, jnp.full((1, WIDE - layer_rows), -1, jnp.int32)], axis=1)
        index = jnp.concatenate(
            [
                jnp.where(bottom, none, to_layer),
                jnp.where(first, none, mine[:, :WIDE]),
                jnp.where(last, none, mine[:, WIDE:]),
                jnp.where(jnp.logical_or(bottom, first), none, composed[:, :WIDE]),
                jnp.where(jnp.logical_or(bottom, last), none, composed[:, WIDE:]),
            ],
            axis=1,
        )
        set_hot(index, halo_hot, halo_mask)

    def part(ref, phase, number):
        return ref.at[phase, :, pl.ds(number * WIDE, WIDE)]

    def pass_token(number):
        for device in tokens[number]:
            pl.semaphore_signal(token_sems.at[number], inc=1, device_id=device, device_id_type=MESH)

    def send(phase, number, segment, device, valid):
        @pl.when(valid)
        def _():
            remote(
                part(sent, phase, number),
                part(received, phase, segment),
                phase_send.at[phase],
                phase_recv.at[phase],
                device,
            )

    def await_segments(phase, sem, count):
        for number in (1, 2, 3, 5):

            @pl.when(count == number)
            def _():
                moved = received.at[phase, :, pl.ds(0, number * WIDE)]
                pltpu.make_async_copy(moved, moved, sem.at[phase]).wait()

    def collect(phase, impulse, ready=None, between=None):
        far_terms = far_jac[0] * impulse[0] + far_jac[1] * impulse[1] + far_jac[2] * impulse[2]
        far_terms = halves(far_terms)
        leaving = scatter(far_terms, (2, 3, 4), far_hot, far_mask)
        for number in range(3):
            sent[phase, :, number * WIDE : (number + 1) * WIDE] = leaving[number]
        send(phase, 1, 4, (above, lower), jnp.logical_and(has_above, has_lower))
        send(phase, 2, 3, (above, higher), jnp.logical_and(has_above, has_higher))
        send(phase, 1, 2, (g, lower), has_lower)
        send(phase, 2, 1, (g, higher), has_higher)
        send(phase, 0, 0, (above, x), has_above)
        if ready is not None:
            ready()
        near_terms = near_jac[0] * impulse[0] + near_jac[1] * impulse[1] + near_jac[2] * impulse[2]
        near_tiles = scatter(halves(near_terms), (0, 1), near_hot, near_mask)
        far_tiles = scatter(far_terms, (0, 1), far_hot, far_mask)
        if between is not None:
            between()
        await_segments(phase, phase_recv, downward)
        halo_tiles = scatter(halves(received[phase]), (0, 1), halo_hot, halo_mask)
        return jnp.concatenate(
            [far_tiles[i] + near_tiles[i] + halo_tiles[i] for i in range(2)], axis=1
        )

    def rows_of(phase, velocity):
        own_tiles = [velocity[:, :WIDE], velocity[:, WIDE:]]
        sent[phase] = gather(own_tiles, range(2), halo_hot, halo_mask)
        send(phase, 3, 3, (below, lower), jnp.logical_and(has_below, has_lower))
        send(phase, 4, 4, (below, higher), jnp.logical_and(has_below, has_higher))
        send(phase, 1, 1, (g, lower), has_lower)
        send(phase, 2, 2, (g, higher), has_higher)
        send(phase, 0, 0, (below, x), has_below)
        near_rows = gather(own_tiles, range(2), near_hot, near_mask)
        far_rows = gather(own_tiles, range(2), far_hot, far_mask)
        partial = [near_jac[r] * near_rows for r in range(3)]
        await_segments(phase, phase_recv, upward)
        segments = [received[phase, :, i * WIDE : (i + 1) * WIDE] for i in range(5)]
        far_rows = far_rows + gather(
            [segments[0], segments[2] + segments[4], segments[1] + segments[3]], (2, 3, 4), far_hot, far_mask
        )
        return [
            jnp.sum(partial[r] + far_jac[r] * far_rows, axis=0, keepdims=True) for r in range(3)
        ]

    def tree(terms):
        while len(terms) > 1:
            pairs = [a + b for a, b in zip(terms[::2], terms[1::2])]
            terms = pairs + terms[2 * len(pairs) :]
        return terms[0]

    def rows_moved(at, sem, count):
        moved = sum_in.at[at, pl.ds(0, count)]
        pltpu.make_async_copy(moved, moved, sem.at[at]).wait()

    def give(at, slot, device):
        remote(sum_out.at[at], sum_in.at[at, slot], sum_send.at[at], sum_recv.at[at], device)

    def all_sum(iteration, value):
        at = iteration * ROUNDS
        sum_out[at] = value
        within = len(plane)

        @pl.when(odd)
        def _():
            for slot, device in enumerate(plane[:-1]):
                give(at, within + slot, device)
            rows_moved(at, sum_recv, 2 * within - 1)
            sum_out[at + 1] = tree([value] + [sum_in[at, slot] for slot in range(2 * within - 1)])
            for slot, (layer, cell) in enumerate(column):
                give(at + 1, slot, (layer - 1, cell))
                give(at + 1, slot, (layer, cell))
            give(at + 1, len(column), (g - 1, x))
            rows_moved(at + 1, sum_recv, len(column))

        @pl.when(jnp.logical_not(odd))
        def _():
            for slot, device in enumerate(plane):
                give(at, slot, device)
            rows_moved(at + 1, sum_recv, len(column) + 1)
            sum_out[at + 1] = sum_in[at + 1, len(column)]

        return tree([sum_out[at + 1]] + [sum_in[at + 1, slot] for slot in range(len(column))])

    pass_token(0)
    factors = momentum_factors(ITERS)
    current = [alive * impulses_ref[r] for r in range(3)]
    earlier = [alive * previous_ref[r] for r in range(3)]
    guess = [alive * (current[r] + factors[0] * (current[r] - earlier[r])) for r in range(3)]
    for iteration in range(ITERS):
        phase = 3 * iteration
        velocity = free + weights * collect(phase, guess, *((set_near, set_halo) if iteration == 0 else ()))
        if iteration == 0:
            pl.semaphore_wait(token_sems.at[0], len(tokens[0]))
            pass_token(1)
        rows = rows_of(phase + 1, velocity)
        rows[0] = rows[0] + offset
        gradient = [alive * (rows[r] + softness * guess[r]) for r in range(3)]
        squares = gradient[0] * gradient[0] + gradient[1] * gradient[1] + gradient[2] * gradient[2]
        norm = lanes(squares)
        soft = lanes(softness * squares)
        sums = collect(phase + 2, gradient)
        if iteration == 0:
            pl.semaphore_wait(token_sems.at[1], len(tokens[1]))
        curve = jnp.sum(lanes(weights * sums * sums), axis=0, keepdims=True) + soft
        value = all_sum(iteration, jnp.concatenate([norm, curve], axis=0))
        total = jnp.sum(value, axis=1, keepdims=True)
        step_size = total[0:1] / (total[1:2] + EPSILON)
        moved = [guess[r] - step_size * gradient[r] for r in range(3)]
        updated = [alive * v for v in cone_project(moved[0], moved[1], moved[2], friction)]
        if iteration + 1 < ITERS:
            guess = [
                alive * (updated[r] + factors[iteration + 1] * (updated[r] - current[r]))
                for r in range(3)
            ]
        current = updated
    for r in range(3):
        impulses_out[r] = current[r]
    final = free + weights * collect(PHASES - 1, current)
    for j in range(6):
        velocity_out[j] = final[j : j + 1, :]

    @pl.when(has_above)
    def _():
        pltpu.make_async_copy(side_out, side_out, side_sems.at[0]).wait()

    for phase in range(PHASES):
        await_segments(phase, phase_send, downward if phase in SPREADS else upward)
    for iteration in range(ITERS):
        at = iteration * ROUNDS

        @pl.when(odd)
        def _():
            rows_moved(at, sum_send, len(plane) - 1)
            rows_moved(at + 1, sum_send, 2 * len(column) + 1)

        @pl.when(jnp.logical_not(odd))
        def _():
            rows_moved(at, sum_send, len(plane))


def solution(mesh):
    layers, cells = mesh.shape["gz"], mesh.shape["xy"]
    depth = 16

    def on_device(
        velocity_free,
        inverse_mass,
        jacobian,
        impulses,
        previous_impulses,
        compliance,
        offset,
        friction,
        body_near,
        body_far,
        block_counts,
        layer_send,
        side_send,
    ):
        own = velocity_free.shape[3]
        contacts = jacobian.shape[3]
        vmem = pl.BlockSpec(memory_space=pltpu.VMEM)
        sums = ITERS * ROUNDS
        partners = max(layers * (cells // depth), depth) - 1
        operands = (
            velocity_free.reshape(6, 1, own),
            inverse_mass[0, 0],
            jacobian.reshape(36 * contacts // 128, 128),
            impulses.reshape(3, 1, contacts),
            previous_impulses.reshape(3, 1, contacts),
            compliance[0],
            offset[0],
            friction[0],
            body_near[0],
            body_far[0],
            block_counts[0],
            layer_send[0],
            side_send[0, 0],
        )
        outs = pl.pallas_call(
            functools.partial(kernel, layers, cells, depth),
            out_shape=(
                jax.ShapeDtypeStruct((3, 1, contacts), F32),
                jax.ShapeDtypeStruct((6, 1, own), F32),
            ),
            in_specs=[pl.BlockSpec(memory_space=pl.ANY)] * 13,
            out_specs=(vmem, vmem),
            scratch_shapes=[
                pltpu.VMEM((WIDE, contacts), BF16),
                pltpu.VMEM((2, 16, contacts), BF16),
                pltpu.VMEM((WIDE, contacts), BF16),
                pltpu.VMEM((5, 16, contacts), BF16),
                pltpu.VMEM((WIDE, 5 * WIDE), BF16),
                pltpu.VMEM((2, 16, 5 * WIDE), BF16),
                pltpu.VMEM((3, 8, contacts), F32),
                pltpu.VMEM((3, 8, contacts), F32),
                pltpu.VMEM((8, 2 * WIDE), F32),
                pltpu.VMEM((8, 2 * WIDE), F32),
                pltpu.VMEM((PHASES, 8, 5 * WIDE), F32),
                pltpu.VMEM((PHASES, 8, 5 * WIDE), F32),
                pltpu.VMEM((sums, 2, 128), F32),
                pltpu.VMEM((sums, partners, 2, 128), F32),
                pltpu.SemaphoreType.DMA((2,)),
                pltpu.SemaphoreType.DMA((PHASES,)),
                pltpu.SemaphoreType.DMA((PHASES,)),
                pltpu.SemaphoreType.DMA((sums,)),
                pltpu.SemaphoreType.DMA((sums,)),
                pltpu.SemaphoreType.REGULAR((2,)),
                *[
                    pltpu.VMEM((v.shape[0] + 4 * contacts // 128, 128), F32) if v is operands[2] else pltpu.VMEM(v.shape, v.dtype)
                    for v in operands
                ],
                pltpu.SemaphoreType.DMA((len(operands),)),
            ],
            compiler_params=pltpu.CompilerParams(
                collective_id=0, has_side_effects=True, vmem_limit_bytes=56 << 20
            ),
        )(*operands)
        return outs[0].reshape(1, 1, 3, contacts), outs[1].reshape(1, 1, 6, own)

    field = P("gz", "xy", None, None)
    line = P("gz", "xy", None)
    return jax.shard_map(
        on_device,
        mesh=mesh,
        in_specs=(field,) * 5 + (line,) * 7 + (field,),
        out_specs=(field, field),
        check_vma=False,
    )
```
